256 devices in a mesh: chain: 8 (over y, core), sector: 32 (over x, z).
Axes of the slice: x: 4, y: 4, z: 8, core: 2. Of those that a mesh axis runs over, the one named last changes fastest.
Arguments:
- site_tensors: bfloat16 [16, 32, 128, 4, 128], P('chain', 'sector'), may hold values from -0.5 to 0.5
- mpo: bfloat16 [16, 42, 42, 4, 4], P('chain'), may hold values from -0.75 to 0.75
- left_in: bfloat16 [8, 32, 42, 128, 128], P('chain', 'sector'), may hold values from -6 to 6
- right_in: bfloat16 [8, 32, 42, 128, 128], P('chain', 'sector'), may hold values from -6 to 6
- tile_rows: int32 [17, 32], replicated, may hold values from 32 to 128
Outputs:
- left_envs: bfloat16 [16, 32, 42, 128, 128], P('chain', 'sector')
- right_envs: bfloat16 [16, 32, 42, 128, 128], P('chain', 'sector')
- left_edge: bfloat16 [8, 32, 42, 128, 128], P('chain', 'sector')
The draws below stay inside these ranges and needn't reach their ends.
All inputs are finite; a program needn't handle non-finite values.
Results may differ from the reference program's by a relative error of at most 0.009.
Values may be sent and summed in bfloat16 or wider, within the bound.
A program may use at most 128 MiB of HBM per device.

```python
import jax
import jax.numpy as jnp
from jax import lax

W = 42
TILE = 128
PHYS = 4
SD = 2
TILES = 32
SITES = 16
BONDS = 17
N_CHAIN = 8


def plant(entries, key, smallest, largest):
    longest = entries.shape.index(max(entries.shape))
    spots = []
    for shift in (0, 1):
        where = [jax.random.randint(jax.random.fold_in(key, axis), (), 0, length) for axis, length in enumerate(entries.shape)]
        where[longest] = (where[longest] + shift) % entries.shape[longest]
        spots.append(tuple(where))
    return entries.at[spots[0]].set(smallest).at[spots[1]].set(largest)


def block_scale(stream_key, extent, split, smallest, high):
    factor_of = 1.0
    for axis_at, blocks in split:
        steps = jax.random.uniform(jax.random.fold_in(jax.random.fold_in(stream_key, 6), axis_at), (blocks,), jnp.float32, smallest / len(split), high / len(split))
        factor_of = factor_of * jnp.repeat(jnp.exp(steps), extent[axis_at] // blocks).reshape((-1,) + (1,) * (len(extent) - 1 - axis_at))
    return factor_of


def noise(key, extent, scale, bound, split=(), kind=jnp.bfloat16):
    values = scale * jax.random.normal(key, extent, jnp.float32)
    if split:
        values = values * block_scale(key, extent, split, -0.22, 0.18)
    return jnp.clip(values, -bound, bound).astype(kind)


def setup_inputs(seed: int = 0) -> dict:
    streams_of = jax.random.split(jax.random.key(seed), 6)
    site_tensors = noise(streams_of[0], (SITES, TILES, TILE, PHYS, TILE), TILE ** -0.5, 0.5, ((0, 8), (1, 32)))
    mpo = noise(streams_of[1], (SITES, W, W, PHYS, PHYS), (3 * W // 2) ** -0.5, 0.75, ((0, 8),))
    left_in = noise(streams_of[2], (N_CHAIN, TILES, W, TILE, TILE), 1.0, 6.0, ((0, 8), (1, 32)))
    right_in = noise(streams_of[3], (N_CHAIN, TILES, W, TILE, TILE), 1.0, 6.0, ((0, 8), (1, 32)))
    tile_rows = plant(jax.random.randint(streams_of[4], (BONDS, TILES), TILE // 4, TILE + 1), jax.random.fold_in(streams_of[4], 1), TILE // 4, TILE).astype(jnp.int32)
    return dict(site_tensors=site_tensors, mpo=mpo, left_in=left_in, right_in=right_in, tile_rows=tile_rows)


charge_groups = ((0, 1), (1, 3), (3, 4))


def mask_part(tensor, rows_left, rows_right, lower, upper):
    tile = tensor.shape[0]
    ids = jnp.arange(tile, dtype=jnp.int32)
    keep = (ids[:, None, None] < rows_left) & (ids[None, None, :] < rows_right)
    return jnp.where(keep, tensor[:, lower:upper, :], jnp.zeros((), tensor.dtype))


def left_tile(env, tensor, mpo_site, rows_left, rows_next):
    tile = tensor.shape[0]
    width = env.shape[0]
    full = jnp.concatenate([mask_part(tensor, rows_left, rows_next[n], lo, hi) for n, (lo, hi) in enumerate(charge_groups)], axis=1)
    prod = jnp.dot(env.reshape(width * tile, tile), full.reshape(tile, 4 * tile), preferred_element_type=jnp.float32)
    prod = prod.astype(jnp.bfloat16).reshape(width, tile, 4, tile)
    terms = []
    for lo, hi in charge_groups:
        inner = jnp.einsum("wvst,wxtb->vxsb", mpo_site[:, :, lo:hi, lo:hi].astype(jnp.float32), prod[:, :, lo:hi, :].astype(jnp.float32)).astype(jnp.bfloat16)
        terms.append(jnp.einsum("xsy,vxsb->vyb", full[:, lo:hi, :].astype(jnp.float32), inner.astype(jnp.float32)))
    return terms[0], terms[1], terms[2]


def right_tile(sources, tensor, mpo_site, rows_left, rows_next):
    tile = tensor.shape[0]
    width = sources[0].shape[0]
    total = jnp.zeros((width, tile, tile), jnp.float32)
    for n, (lo, hi) in enumerate(charge_groups):
        part = mask_part(tensor, rows_left, rows_next[n], lo, hi)
        count = hi - lo
        prod = jnp.dot(sources[n].reshape(width * tile, tile), part.reshape(tile * count, tile).T, preferred_element_type=jnp.float32)
        prod = prod.astype(jnp.bfloat16).reshape(width, tile, tile, count)
        inner = jnp.einsum("wust,uyat->wyas", mpo_site[:, :, lo:hi, lo:hi].astype(jnp.float32), prod.astype(jnp.float32)).astype(jnp.bfloat16)
        total = total + jnp.einsum("xsy,wyas->wxa", part.astype(jnp.float32), inner.astype(jnp.float32))
    return total.astype(jnp.bfloat16)


def next_rows(rows_there):
    count = rows_there.shape[0]
    padded = jnp.concatenate([rows_there, jnp.zeros((2,), jnp.int32)])
    return jnp.stack([padded[n:n + count] for n in range(3)], axis=1)


def left_site(env_all, tensors, mpo_site, rows_here, rows_there):
    rows_next = next_rows(rows_there)
    first, second, third = jax.vmap(left_tile, in_axes=(0, 0, None, 0, 0))(env_all, tensors, mpo_site, rows_here, rows_next)
    second = lax.optimization_barrier(second.astype(jnp.bfloat16)).astype(jnp.float32)
    third = lax.optimization_barrier(third.astype(jnp.bfloat16)).astype(jnp.float32)
    moved_one = jnp.concatenate([jnp.zeros_like(second[:1]), second[:-1]], axis=0)
    moved_two = jnp.concatenate([jnp.zeros_like(third[:2]), third[:-2]], axis=0)
    return (first + moved_one + moved_two).astype(jnp.bfloat16)


def right_site(env_all, tensors, mpo_site, rows_here, rows_there):
    rows_next = next_rows(rows_there)
    count = env_all.shape[0]
    padded = jnp.concatenate([env_all, jnp.zeros((2,) + env_all.shape[1:], env_all.dtype)], axis=0)
    sources = (padded[0:count], padded[1:count + 1], padded[2:count + 2])
    return jax.vmap(right_tile, in_axes=(0, 0, None, 0, 0))(sources, tensors, mpo_site, rows_here, rows_next)


def reference(site_tensors, mpo, left_in, right_in, tile_rows):
    lefts = []
    rights = [None] * SITES
    for segment in range(N_CHAIN):
        env = left_in[segment]
        for inner in range(SD):
            site = segment * SD + inner
            env = left_site(env, site_tensors[site], mpo[site], tile_rows[site], tile_rows[site + 1])
            lefts.append(env)
    for segment in range(N_CHAIN):
        env = right_in[segment]
        for inner in reversed(range(SD)):
            site = segment * SD + inner
            env = right_site(env, site_tensors[site], mpo[site], tile_rows[site], tile_rows[site + 1])
            rights[site] = env
    left_envs = jnp.stack(lefts)
    right_envs = jnp.stack(rights)
    left_edge = jnp.concatenate([left_in[:1], left_envs[SD - 1::SD][:N_CHAIN - 1]], axis=0)
    return left_envs, right_envs, left_edge
```

```python
import functools

import jax
import jax.numpy as jnp
from jax import lax
from jax.experimental import pallas as pl
from jax.experimental.pallas import tpu as pltpu
from jax.sharding import PartitionSpec as P

groups = ((0, 1), (1, 3), (3, 4))
SLICES = 4
PITCH_EXTRA = 8
ROWS = 8


def stage_one(width, tile, padded, pitch, src, lhs, mid):
    count = lhs.shape[0] // tile

    def pair(i, carry):
        rhs = jnp.concatenate([src[2 * i], src[2 * i + 1]], axis=1)
        prod = jnp.dot(lhs, rhs, preferred_element_type=jnp.float32)
        for s in range(count):
            for j in range(2):
                row = pl.multiple_of((s * padded + 2 * i + j) * pitch, 8)
                mid[pl.ds(row, tile), :] = prod[
                    s * tile : (s + 1) * tile, j * tile : (j + 1) * tile
                ]
        return carry

    lax.fori_loop(0, width // 2, pair, 0)


def stage_two(tile, padded, pitch, start, rows, mid, mpo_part, fin, out, add):
    count = fin.shape[0] // tile

    def block(i, carry):
        base = start + i * ROWS
        left = []
        for j in range(0, ROWS, 2):
            both = [
                mid[pl.ds(base + j + k, count * padded, stride=pitch), :].astype(
                    jnp.bfloat16
                )
                for k in range(2)
            ]
            inner = jnp.dot(
                mpo_part,
                jnp.concatenate(both, axis=1),
                preferred_element_type=jnp.float32,
            ).astype(jnp.bfloat16)
            for k in range(2):
                left.append(
                    jnp.concatenate(
                        [
                            inner[
                                t * padded : (t + 1) * padded,
                                k * tile : (k + 1) * tile,
                            ]
                            for t in range(count)
                        ],
                        axis=1,
                    )
                )
        prod = jnp.dot(
            jnp.concatenate(left, axis=0), fin, preferred_element_type=jnp.float32
        )
        for j in range(ROWS):
            spot = pl.ds(base + j, padded, stride=pitch)
            value = prod[j * padded : (j + 1) * padded]
            if add:
                value = value + out[spot, :]
            out[spot, :] = value
        return carry

    lax.fori_loop(0, rows // ROWS, block, 0)


def emit(width, pitch, start, rows, acc, other, dst):
    def one(w, carry):
        value = acc[pl.ds(pl.multiple_of(w * pitch + start, 8), rows), :]
        if other is not None:
            value = value + other[w, start : start + rows, :].astype(jnp.float32)
        dst[w, start : start + rows, :] = value.astype(jnp.bfloat16)
        return carry

    lax.fori_loop(0, width, one, 0)


def kernel(
    sizes,
    lin, rin, am, at, ml0, ml1, ml2, mr0, mr1, mr2,
    left_out, right_out, edge_out,
    r_one, r_two, p_send, p_recv, s_send, s_recv,
    mid, acc_one, acc_zero, acc_right,
    send_sem, recv_sem,
):
    chain_count, sector_count, sites, width, tile, padded, pitch = sizes
    chain = lax.axis_index("chain")
    sector = lax.axis_index("sector")
    up = lax.rem(sector + 1, sector_count)
    down = lax.rem(sector + sector_count - 1, sector_count)
    after = lax.rem(chain + 1, chain_count)
    before = lax.rem(chain + chain_count - 1, chain_count)
    rows = tile // SLICES
    ml = (ml0, ml1, ml2)
    mr = (mr0, mr1, mr2)

    barrier = pltpu.get_barrier_semaphore()
    for there in ({"sector": up}, {"sector": down}, {"chain": after}, {"chain": before}):
        pl.semaphore_signal(barrier, inc=1, device_id=there)
    pl.semaphore_wait(barrier, 4)

    def piece(src, dst, stream, c, there):
        cut = (slice(None), pl.ds(c * rows, rows), slice(None))
        return pltpu.make_async_remote_copy(
            src_ref=src.at[cut],
            dst_ref=dst.at[cut],
            send_sem=send_sem.at[stream, c],
            recv_sem=recv_sem.at[stream, c],
            device_id=there,
            device_id_type=pl.DeviceIdType.MESH,
        )

    def lhs_of(mats, site, n):
        lo, hi = groups[n]
        return mats[site, lo:hi].reshape((hi - lo) * tile, tile)

    one = functools.partial(stage_one, width, tile, padded, pitch)
    two = functools.partial(stage_two, tile, padded, pitch)
    out = functools.partial(emit, width, pitch)

    def left_pass(src, site, n, acc):
        one(src, lhs_of(at, site, n), mid)
        two(0, tile, mid, ml[n][site], lhs_of(am, site, n), acc, False)

    def right_pass(src, site, n, add):
        one(src, lhs_of(am, site, n), mid)
        two(0, tile, mid, mr[n][site], lhs_of(at, site, n), acc_right, add)

    copies = []
    zero = jnp.zeros((tile, tile), jnp.float32)
    for s in range(2):
        for w in range(width, padded):
            mid[pl.ds((s * padded + w) * pitch, tile), :] = zero

    left_src = lin
    right_src = rin
    for c in range(SLICES):
        copies.append(piece(rin, r_one.at[0], 0, c, {"sector": down}))
        copies[-1].start()
    own = copies[-SLICES:]
    for step in range(sites):
        base = step * 4
        lsite, rsite = step, sites - 1 - step
        one(left_src, lhs_of(at, lsite, 2), mid)
        firsts = []
        for c in range(SLICES):
            two(c * rows, rows, mid, ml[2][lsite], lhs_of(am, lsite, 2), acc_one, False)
            out(c * rows, rows, acc_one, None, p_send.at[step])
            firsts.append(
                piece(p_send.at[step], p_recv.at[step], base + 1, c, {"sector": up})
            )
            firsts[-1].start()
        if step > 0:
            one(r_two.at[step - 1], lhs_of(am, rsite + 1, 2), mid)
            own = []
            for c in range(SLICES):
                two(
                    c * rows, rows, mid, mr[2][rsite + 1], lhs_of(at, rsite + 1, 2),
                    acc_right, True,
                )
                out(c * rows, rows, acc_right, None, right_out.at[rsite + 1])
                own.append(
                    piece(
                        right_out.at[rsite + 1], r_one.at[step], base, c,
                        {"sector": down},
                    )
                )
                own[-1].start()
            copies += own
            right_src = right_out.at[rsite + 1]
        left_pass(left_src, lsite, 1, acc_one)
        right_pass(right_src, rsite, 0, False)
        seconds, relays = [], []
        for c in range(SLICES):
            firsts[c].wait_recv()
            out(c * rows, rows, acc_one, p_recv.at[step], s_send.at[step])
            seconds.append(
                piece(s_send.at[step], s_recv.at[step], base + 2, c, {"sector": up})
            )
            seconds[-1].start()
            own[c].wait_recv()
            relays.append(
                piece(r_one.at[step], r_two.at[step], base + 3, c, {"sector": down})
            )
            relays[-1].start()
        left_pass(left_src, lsite, 0, acc_zero)
        right_pass(r_one.at[step], rsite, 1, True)
        last = step == sites - 1
        for c in range(SLICES):
            seconds[c].wait_recv()
            out(c * rows, rows, acc_zero, s_recv.at[step], left_out.at[lsite])
            if last:
                edge = piece(left_out.at[lsite], edge_out, 4 * sites, c, {"chain": after})

                @pl.when(chain < chain_count - 1)
                def _(edge=edge):
                    edge.start()

        left_src = left_out.at[lsite]
        for c in range(SLICES):
            relays[c].wait_recv()
        copies += firsts + seconds + relays
    right_pass(r_two.at[sites - 1], 0, 2, True)
    for c in range(SLICES):
        out(c * rows, rows, acc_right, None, right_out.at[0])

    @pl.when(chain == 0)
    def _():
        def keep(w, carry):
            edge_out[w] = lin[w]
            return carry

        lax.fori_loop(0, width, keep, 0)

    for c in range(SLICES):
        edge = piece(left_out.at[sites - 1], edge_out, 4 * sites, c, {"chain": after})

        @pl.when(chain > 0)
        def _(edge=edge):
            edge.wait_recv()

        @pl.when(chain < chain_count - 1)
        def _(edge=edge):
            edge.wait_send()

    for copy in copies:
        copy.wait_send()


def masked(site_tensors, tile_rows, first, position, count):
    sites, tile, phys = site_tensors.shape[:3]
    ids = lax.iota(jnp.int32, tile)
    padded = jnp.pad(tile_rows, ((0, 0), (0, 2)))
    window = lax.dynamic_slice(padded, (first, position), (sites + 1, 3))
    left = window[:sites, 0]
    right = jnp.stack([window[1:, n] for n in (0, 1, 1, 2)], axis=1)
    keep = (ids[None, :, None, None] < left[:, None, None, None]) & (
        ids[None, None, None, :] < right[:, None, :, None]
    )
    return jnp.where(keep, site_tensors, jnp.zeros((), site_tensors.dtype))


def shards(chain_count, sector_count, site_tensors, mpo, left_in, right_in, tile_rows):
    chain = lax.axis_index("chain")
    sector = lax.axis_index("sector")
    sites, _, tile, _, _ = site_tensors.shape
    width = mpo.shape[1]
    padded = -(-width // 16) * 16
    pitch = tile + PITCH_EXTRA
    kept = masked(site_tensors[:, 0], tile_rows, chain * sites, sector, sector_count)
    am = kept.transpose(0, 2, 1, 3)
    at = kept.transpose(0, 2, 3, 1)
    extra = padded - width
    wide = jnp.pad(mpo, ((0, 0), (0, extra), (0, extra), (0, 0), (0, 0)))
    ml, mr = [], []
    for lo, hi in groups:
        part = wide[..., lo:hi, lo:hi]
        side = (hi - lo) * padded
        ml.append(part.transpose(0, 4, 2, 3, 1).reshape(sites, side, side))
        mr.append(part.transpose(0, 4, 1, 3, 2).reshape(sites, side, side))
    env = (width, tile, tile)
    sizes = (chain_count, sector_count, sites, width, tile, padded, pitch)
    vmem = pl.BlockSpec(memory_space=pltpu.VMEM)
    streams = 4 * sites + 1
    left, right, edge = pl.pallas_call(
        functools.partial(kernel, sizes),
        out_shape=(
            jax.ShapeDtypeStruct((sites,) + env, jnp.bfloat16),
            jax.ShapeDtypeStruct((sites,) + env, jnp.bfloat16),
            jax.ShapeDtypeStruct(env, jnp.bfloat16),
        ),
        in_specs=[vmem] * 10,
        out_specs=[vmem] * 3,
        scratch_shapes=[pltpu.VMEM((sites,) + env, jnp.bfloat16)] * 6
        + [
            pltpu.VMEM((2 * padded * pitch, tile), jnp.float32),
            pltpu.VMEM((padded * pitch, tile), jnp.float32),
            pltpu.VMEM((padded * pitch, tile), jnp.float32),
            pltpu.VMEM((padded * pitch, tile), jnp.float32),
            pltpu.SemaphoreType.DMA((streams, SLICES)),
            pltpu.SemaphoreType.DMA((streams, SLICES)),
        ],
        compiler_params=pltpu.CompilerParams(
            collective_id=0, has_side_effects=True, vmem_limit_bytes=67043328
        ),
    )(left_in[0, 0], right_in[0, 0], am, at, *ml, *mr)
    return left[:, None], right[:, None], edge[None, None]


def solution(mesh):
    envs = P("chain", "sector", None, None, None)
    return jax.shard_map(
        functools.partial(shards, mesh.shape["chain"], mesh.shape["sector"]),
        mesh=mesh,
        in_specs=(envs, P("chain", None, None, None, None), envs, envs, P()),
        out_specs=(envs, envs, envs),
        check_vma=False,
    )
```

```python
import functools

import jax
import jax.numpy as jnp
from jax import lax
from jax.experimental import pallas as pl
from jax.experimental.pallas import tpu as pltpu
from jax.sharding import PartitionSpec as P

groups = ((0, 1), (1, 3), (3, 4))
charge = (0, 1, 1, 2)
SLICES = 4
PITCH_EXTRA = 8
ROWS = 16
PAIRS = 3


def stage_one(width, tile, padded, pitch, src, lhs, mid):
    count = lhs.shape[0] // tile
    pairs = width // 2
    unroll = max(n for n in range(1, PAIRS + 1) if pairs % n == 0)

    def body(i, carry):
        for k in range(unroll):
            w = (i * unroll + k) * 2
            rhs = jnp.concatenate([src[w], src[w + 1]], axis=1)
            prod = jnp.dot(lhs, rhs, preferred_element_type=jnp.float32)
            for s in range(count):
                for j in range(2):
                    row = pl.multiple_of((s * padded + w + j) * pitch, 8)
                    mid[pl.ds(row, tile), :] = prod[
                        s * tile : (s + 1) * tile, j * tile : (j + 1) * tile
                    ]
        return carry

    lax.fori_loop(0, pairs // unroll, body, 0)


def stage_two(tile, padded, pitch, start, rows, mid, mpo_part, fin, out, add):
    count = fin.shape[0] // tile

    def block(i, carry):
        base = start + i * ROWS
        left = []
        for j in range(0, ROWS, 2):
            both = [
                mid[pl.ds(base + j + k, count * padded, stride=pitch), :].astype(
                    jnp.bfloat16
                )
                for k in range(2)
            ]
            inner = jnp.dot(
                mpo_part,
                jnp.concatenate(both, axis=1),
                preferred_element_type=jnp.float32,
            ).astype(jnp.bfloat16)
            for k in range(2):
                left.append(
                    jnp.concatenate(
                        [
                            inner[
                                t * padded : (t + 1) * padded,
                                k * tile : (k + 1) * tile,
                            ]
                            for t in range(count)
                        ],
                        axis=1,
                    )
                )
        prod = jnp.dot(
            jnp.concatenate(left, axis=0), fin, preferred_element_type=jnp.float32
        )
        for j in range(ROWS):
            spot = pl.ds(base + j, padded, stride=pitch)
            value = prod[j * padded : (j + 1) * padded]
            if add:
                value = value + out[spot, :]
            out[spot, :] = value
        return carry

    lax.fori_loop(0, rows // ROWS, block, 0)


def emit(width, pitch, start, rows, acc, other, dst):
    def one(i, carry):
        for k in range(2):
            w = 2 * i + k
            value = acc[pl.ds(pl.multiple_of(w * pitch + start, 8), rows), :]
            if other is not None:
                value = value + other[w, start : start + rows, :].astype(jnp.float32)
            dst[w, start : start + rows, :] = value.astype(jnp.bfloat16)
        return carry

    lax.fori_loop(0, width // 2, one, 0)


def kernel(
    sizes,
    rows_ref, a_in, m_in, lin_hbm, rin_hbm,
    left_out, right_out, edge_out,
    lin, rin, r_one, r_two, p_send, p_recv, s_send, s_recv,
    mid, acc_one, acc_zero, acc_right, am, at, m_one, m_two, a_wide, m_wide,
    send_sem, recv_sem, load_sem,
):
    chain_count, sector_count, sites, width, tile, padded, pitch = sizes
    chain = lax.axis_index("chain")
    sector = lax.axis_index("sector")
    up = lax.rem(sector + 1, sector_count)
    down = lax.rem(sector + sector_count - 1, sector_count)
    after = lax.rem(chain + 1, chain_count)
    before = lax.rem(chain + chain_count - 1, chain_count)
    rows = tile // SLICES

    barrier = pltpu.get_barrier_semaphore()
    for there in ({"sector": up}, {"sector": down}, {"chain": after}, {"chain": before}):
        pl.semaphore_signal(barrier, inc=1, device_id=there)
    load_left = pltpu.make_async_copy(lin_hbm, lin, load_sem.at[0])
    load_right = pltpu.make_async_copy(rin_hbm, rin, load_sem.at[1])
    load_left.start()
    load_right.start()

    def piece(src, dst, stream, c, there):
        cut = (slice(None), pl.ds(c * rows, rows), slice(None))
        return pltpu.make_async_remote_copy(
            src_ref=src.at[cut],
            dst_ref=dst.at[cut],
            send_sem=send_sem.at[stream, c],
            recv_sem=recv_sem.at[stream, c],
            device_id=there,
            device_id_type=pl.DeviceIdType.MESH,
        )

    ids_a = lax.broadcasted_iota(jnp.int32, (tile, tile), 0)
    ids_b = lax.broadcasted_iota(jnp.int32, (tile, tile), 1)

    def widen(site):
        a_wide[site] = a_in[site].astype(jnp.float32)
        m_wide[site, 0 : 16 * width, 0:width] = m_in[site].astype(jnp.float32)

    def prepare_tensor(site, t):
        bond = chain * sites + site
        there = sector + charge[t]
        seen = rows_ref[bond + 1, jnp.minimum(there, sector_count - 1)]
        high = jnp.where(there < sector_count, seen, 0)
        keep = (ids_a < rows_ref[bond, sector]) & (ids_b < high)
        value = jnp.where(keep, a_wide[site, pl.ds(t, tile, stride=4), :], 0.0)
        am[site, t] = value.astype(jnp.bfloat16)
        at[site, t] = value.T.astype(jnp.bfloat16)

    def corner(side, site, s, t):
        value = m_wide[site, pl.ds(4 * s + t, padded, stride=16), :]
        if side == 0:
            full = jnp.concatenate(
                [value, jnp.zeros((tile - padded, tile), jnp.float32)], axis=0
            )
            value = full.T[:padded]
        return value

    def prepare_mpo(side, site, n):
        lo, hi = groups[n]
        for t in range(lo, hi):
            value = corner(side, site, lo, t)
            for s in range(lo + 1, hi):
                value = value + pltpu.roll(
                    corner(side, site, s, t), (s - lo) * padded, 1
                )
            value = value.astype(jnp.bfloat16)
            if n == 1:
                m_two[side, site, (t - lo) * padded : (t - lo + 1) * padded] = value
            else:
                m_one[side, site, n // 2] = value

    def mpo_of(side, site, n):
        if n == 1:
            return m_two[side, site, :, : 2 * padded]
        return m_one[side, site, n // 2, :, :padded]

    def stack_of(mats, site, n):
        lo, hi = groups[n]
        return mats[site, lo:hi].reshape((hi - lo) * tile, tile)

    one = functools.partial(stage_one, width, tile, padded, pitch)
    two = functools.partial(stage_two, tile, padded, pitch)
    out = functools.partial(emit, width, pitch)

    def first(side, src, site, n):
        one(src, stack_of(am if side else at, site, n), mid)

    def second(side, site, n, start, count, acc, add):
        two(
            start, count, mid, mpo_of(side, site, n),
            stack_of(at if side else am, site, n), acc, add,
        )

    def both(side, src, site, n, acc, add):
        first(side, src, site, n)
        second(side, site, n, 0, tile, acc, add)

    m_wide[...] = jnp.zeros_like(m_wide)
    zero = jnp.zeros((tile, tile), jnp.float32)
    for s in range(2):
        for w in range(width, padded):
            mid[pl.ds((s * padded + w) * pitch, tile), :] = zero
    pl.semaphore_wait(barrier, 4)

    copies = []
    for c in range(SLICES):
        copies.append(piece(rin_hbm, r_one.at[0], 0, c, {"sector": down}))
        copies[-1].start()
    own = copies[-SLICES:]
    widen(0)
    prepare_tensor(0, 3)
    prepare_mpo(0, 0, 2)
    load_left.wait()
    left_src = lin
    right_src = rin
    for step in range(sites):
        base = step * 4
        lsite, rsite = step, sites - 1 - step
        first(0, left_src, lsite, 2)
        firsts = []
        own = own if step == 0 else []
        for c in range(SLICES):
            second(0, lsite, 2, c * rows, rows, acc_one, False)
            out(c * rows, rows, acc_one, None, p_send.at[step])
            firsts.append(
                piece(p_send.at[step], p_recv.at[step], base + 1, c, {"sector": up})
            )
            firsts[-1].start()
        if step > 0:
            first(1, r_two.at[step - 1], rsite + 1, 2)
            for c in range(SLICES):
                second(1, rsite + 1, 2, c * rows, rows, acc_right, True)
                out(c * rows, rows, acc_right, None, right_out.at[rsite + 1])
                own.append(
                    piece(
                        right_out.at[rsite + 1], r_one.at[step], base, c,
                        {"sector": down},
                    )
                )
                own[-1].start()
            copies += own
            right_src = right_out.at[rsite + 1]
        if step == 0:
            for t in range(3):
                prepare_tensor(0, t)
            for site in range(1, sites):
                widen(site)
                for t in range(4):
                    prepare_tensor(site, t)
            for side in range(2):
                for site in range(sites):
                    for n in range(3):
                        if (side, site, n) != (0, 0, 2):
                            prepare_mpo(side, site, n)
        both(0, left_src, lsite, 1, acc_one, False)
        if step == 0:
            load_right.wait()
        both(1, right_src, rsite, 0, acc_right, False)
        seconds, relays = [], []
        for c in range(SLICES):
            firsts[c].wait_recv()
            out(c * rows, rows, acc_one, p_recv.at[step], s_send.at[step])
            seconds.append(
                piece(s_send.at[step], s_recv.at[step], base + 2, c, {"sector": up})
            )
            seconds[-1].start()
            own[c].wait_recv()
            relays.append(
                piece(r_one.at[step], r_two.at[step], base + 3, c, {"sector": down})
            )
            relays[-1].start()
        both(0, left_src, lsite, 0, acc_zero, False)
        both(1, r_one.at[step], rsite, 1, acc_right, True)
        last = step == sites - 1
        for c in range(SLICES):
            seconds[c].wait_recv()
            out(c * rows, rows, acc_zero, s_recv.at[step], left_out.at[lsite])
            if last:
                edge = piece(left_out.at[lsite], edge_out, 4 * sites, c, {"chain": after})

                @pl.when(chain < chain_count - 1)
                def _(edge=edge):
                    edge.start()

        left_src = left_out.at[lsite]
        for c in range(SLICES):
            relays[c].wait_recv()
        copies += firsts + seconds + relays
    both(1, r_two.at[sites - 1], 0, 2, acc_right, True)
    for c in range(SLICES):
        out(c * rows, rows, acc_right, None, right_out.at[0])

    @pl.when(chain == 0)
    def _():
        def keep(w, carry):
            edge_out[w] = lin[w]
            return carry

        lax.fori_loop(0, width, keep, 0)

    for c in range(SLICES):
        edge = piece(left_out.at[sites - 1], edge_out, 4 * sites, c, {"chain": after})

        @pl.when(chain > 0)
        def _(edge=edge):
            edge.wait_recv()

        @pl.when(chain < chain_count - 1)
        def _(edge=edge):
            edge.wait_send()

    for copy in copies:
        copy.wait_send()


def shards(chain_count, sector_count, site_tensors, mpo, left_in, right_in, tile_rows):
    sites, _, tile, phys, _ = site_tensors.shape
    width = mpo.shape[1]
    padded = -(-width // 16) * 16
    pitch = tile + PITCH_EXTRA
    tensors = site_tensors.reshape(sites, tile * phys, tile)
    flat_mpo = mpo.transpose(0, 1, 3, 4, 2).reshape(sites, width * 16, width)
    env = (width, tile, tile)
    sizes = (chain_count, sector_count, sites, width, tile, padded, pitch)
    vmem = pl.BlockSpec(memory_space=pltpu.VMEM)
    hbm = pl.BlockSpec(memory_space=pl.ANY)
    streams = 4 * sites + 1
    left, right, edge = pl.pallas_call(
        functools.partial(kernel, sizes),
        out_shape=(
            pltpu.VMEM((sites,) + env, jnp.bfloat16),
            pltpu.VMEM((sites,) + env, jnp.bfloat16),
            pltpu.VMEM(env, jnp.bfloat16),
        ),
        in_specs=[pl.BlockSpec(memory_space=pltpu.SMEM), vmem, vmem, hbm, hbm],
        out_specs=[vmem] * 3,
        scratch_shapes=[pltpu.VMEM(env, jnp.bfloat16)] * 2
        + [pltpu.VMEM((sites,) + env, jnp.bfloat16)] * 6
        + [
            pltpu.VMEM((2 * padded * pitch, tile), jnp.float32),
            pltpu.VMEM((padded * pitch, tile), jnp.float32),
            pltpu.VMEM((padded * pitch, tile), jnp.float32),
            pltpu.VMEM((padded * pitch, tile), jnp.float32),
            pltpu.VMEM((sites, phys, tile, tile), jnp.bfloat16),
            pltpu.VMEM((sites, phys, tile, tile), jnp.bfloat16),
            pltpu.VMEM((2, sites, 2, padded, tile), jnp.bfloat16),
            pltpu.VMEM((2, sites, 2 * padded, tile), jnp.bfloat16),
            pltpu.VMEM((sites, phys * tile, tile), jnp.float32),
            pltpu.VMEM((sites, 16 * padded, tile), jnp.float32),
            pltpu.SemaphoreType.DMA((streams, SLICES)),
            pltpu.SemaphoreType.DMA((streams, SLICES)),
            pltpu.SemaphoreType.DMA((2,)),
        ],
        compiler_params=pltpu.CompilerParams(
            collective_id=0, has_side_effects=True, vmem_limit_bytes=52 << 20
        ),
    )(tile_rows, tensors, flat_mpo, left_in[0, 0], right_in[0, 0])
    return left[:, None], right[:, None], edge[None, None]


def solution(mesh):
    envs = P("chain", "sector", None, None, None)
    return jax.shard_map(
        functools.partial(shards, mesh.shape["chain"], mesh.shape["sector"]),
        mesh=mesh,
        in_specs=(envs, P("chain", None, None, None, None), envs, envs, P()),
        out_specs=(envs, envs, envs),
        check_vma=False,
    )
```

```python
import functools

import jax
import jax.numpy as jnp
from jax import lax
from jax.experimental import pallas as pl
from jax.experimental.pallas import tpu as pltpu
from jax.sharding import PartitionSpec as P

groups = ((0, 1), (1, 3), (3, 4))
charge = (0, 1, 1, 2)
SLICES = 4
SPAN = 6
PITCH_EXTRA = 8
ROWS = 16
PAIRS = 3


def stage_one(tile, padded, pitch, start, width, src, lhs, mid):
    count = lhs.shape[0] // tile
    pairs = width // 2
    unroll = max(n for n in range(1, PAIRS + 1) if pairs % n == 0)

    def body(i, carry):
        for k in range(unroll):
            w = start + (i * unroll + k) * 2
            rhs = jnp.concatenate([src[w], src[w + 1]], axis=1)
            prod = jnp.dot(lhs, rhs, preferred_element_type=jnp.float32)
            for s in range(count):
                for j in range(2):
                    row = pl.multiple_of((s * padded + w + j) * pitch, 8)
                    mid[pl.ds(row, tile), :] = prod[
                        s * tile : (s + 1) * tile, j * tile : (j + 1) * tile
                    ]
        return carry

    lax.fori_loop(0, pairs // unroll, body, 0)


def stage_two(tile, padded, pitch, start, rows, mid, mpo_part, fin, out, add):
    count = fin.shape[0] // tile

    def block(i, carry):
        base = start + i * ROWS
        left = []
        for j in range(0, ROWS, 2):
            both = [
                mid[pl.ds(base + j + k, count * padded, stride=pitch), :].astype(
                    jnp.bfloat16
                )
                for k in range(2)
            ]
            inner = jnp.dot(
                mpo_part,
                jnp.concatenate(both, axis=1),
                preferred_element_type=jnp.float32,
            ).astype(jnp.bfloat16)
            for k in range(2):
                left.append(
                    jnp.concatenate(
                        [
                            inner[
                                t * padded : (t + 1) * padded,
                                k * tile : (k + 1) * tile,
                            ]
                            for t in range(count)
                        ],
                        axis=1,
                    )
                )
        prod = jnp.dot(
            jnp.concatenate(left, axis=0), fin, preferred_element_type=jnp.float32
        )
        for j in range(ROWS):
            spot = pl.ds(base + j, padded, stride=pitch)
            value = prod[j * padded : (j + 1) * padded]
            if add:
                value = value + out[spot, :]
            out[spot, :] = value
        return carry

    lax.fori_loop(0, rows // ROWS, block, 0)


def ket_first(width, padded, pitch, start, rows, src, fin, mpo_part, mid, inner):
    group = max(n for n in range(1, 7) if width % n == 0)

    def body(i, carry):
        first = i * group
        block = src[pl.ds(first, group), start : start + rows, :]
        prod = jnp.dot(
            block.reshape(group * rows, block.shape[2]),
            fin,
            preferred_element_type=jnp.float32,
        )
        for k in range(group):
            row = pl.multiple_of((first + k) * pitch + start, 8)
            mid[pl.ds(row, rows), :] = prod[k * rows : (k + 1) * rows]
        return carry

    lax.fori_loop(0, width // group, body, 0)
    tile = fin.shape[1]

    def block(i, carry):
        for j in range(0, ROWS, 2):
            base = start + i * ROWS + j
            both = [
                mid[pl.ds(base + k, padded, stride=pitch), :].astype(jnp.bfloat16)
                for k in range(2)
            ]
            prod = jnp.dot(
                mpo_part,
                jnp.concatenate(both, axis=1),
                preferred_element_type=jnp.float32,
            )
            for k in range(2):
                inner[pl.ds(base + k, padded, stride=pitch), :] = prod[
                    :, k * tile : (k + 1) * tile
                ]
        return carry

    lax.fori_loop(0, rows // ROWS, block, 0)


def bra_last(tile, pitch, start, width, inner, lhs, acc, dst):
    for w in range(start, start + width, 2):
        rows = [pl.ds((w + k) * pitch, tile) for k in range(2)]
        rhs = jnp.concatenate(
            [inner[row, :].astype(jnp.bfloat16) for row in rows], axis=1
        )
        prod = jnp.dot(lhs, rhs, preferred_element_type=jnp.float32)
        for k in range(2):
            value = prod[:, k * tile : (k + 1) * tile]
            if acc is not None:
                value = value + acc[rows[k], :]
            dst[w + k] = value.astype(jnp.bfloat16)


def emit(pitch, wide, tall, acc, other, dst):
    first, width = wide
    start, rows = tall

    def one(i, carry):
        for k in range(2):
            w = first + 2 * i + k
            value = acc[pl.ds(pl.multiple_of(w * pitch + start, 8), rows), :]
            if other is not None:
                value = value + other[w, start : start + rows, :].astype(jnp.float32)
            dst[w, start : start + rows, :] = value.astype(jnp.bfloat16)
        return carry

    lax.fori_loop(0, width // 2, one, 0)


def in_order(*lists):
    spots = []
    for at, (count, act) in enumerate(lists):
        spots += [((c + 1) / count, at, c, act) for c in range(count)]
    for _, _, c, act in sorted(spots, key=lambda spot: spot[:3]):
        act(c)


def kernel(
    sizes,
    rows_ref, a_hbm, m_hbm, lin_hbm, rin_hbm,
    left_out, right_out, edge_out,
    lin, rin, r_one, r_two, p_send, p_recv, s_send, s_recv,
    mid, mid_bra, mid_ket, inner, acc_one, acc_zero, acc_right,
    am, at, m_one, m_two, a_in, m_in, a_wide, m_wide,
    send_sem, recv_sem, load_sem,
):
    chain_count, sector_count, sites, width, tile, padded, pitch = sizes
    chain = lax.axis_index("chain")
    sector = lax.axis_index("sector")
    up = lax.rem(sector + 1, sector_count)
    down = lax.rem(sector + sector_count - 1, sector_count)
    after = lax.rem(chain + 1, chain_count)
    before = lax.rem(chain + chain_count - 1, chain_count)
    rows = tile // SLICES
    chunks = width // SPAN

    barrier = pltpu.get_barrier_semaphore()
    for there in ({"sector": up}, {"sector": down}, {"chain": after}, {"chain": before}):
        pl.semaphore_signal(barrier, inc=1, device_id=there)
    loads = [
        pltpu.make_async_copy(src, dst, load_sem.at[i])
        for i, (src, dst) in enumerate(
            ((a_hbm, a_in), (m_hbm, m_in), (lin_hbm, lin), (rin_hbm, rin))
        )
    ]
    for load in loads:
        load.start()
    keep_edge = pltpu.make_async_copy(lin_hbm, edge_out, load_sem.at[4])

    @pl.when(chain == 0)
    def _():
        keep_edge.start()

    def piece(form, src, dst, stream, c, there):
        if form == "bra":
            cut = (slice(None), pl.ds(c * rows, rows), slice(None))
        else:
            cut = (pl.ds(c * SPAN, SPAN), slice(None), slice(None))
        return pltpu.make_async_remote_copy(
            src_ref=src.at[cut],
            dst_ref=dst.at[cut],
            send_sem=send_sem.at[stream, c],
            recv_sem=recv_sem.at[stream, c],
            device_id=there,
            device_id_type=pl.DeviceIdType.MESH,
        )

    def pieces(form, src, dst, stream, there):
        count = SLICES if form == "bra" else chunks
        return [piece(form, src, dst, stream, c, there) for c in range(count)]

    ids_a = lax.broadcasted_iota(jnp.int32, (tile, tile), 0)
    ids_b = lax.broadcasted_iota(jnp.int32, (tile, tile), 1)

    def widen(site):
        a_wide[site] = a_in[site].astype(jnp.float32)
        m_wide[site, 0 : 16 * width, 0:width] = m_in[site].astype(jnp.float32)

    def prepare_tensor(site, t):
        bond = chain * sites + site
        there = sector + charge[t]
        seen = rows_ref[bond + 1, jnp.minimum(there, sector_count - 1)]
        high = jnp.where(there < sector_count, seen, 0)
        keep = (ids_a < rows_ref[bond, sector]) & (ids_b < high)
        value = jnp.where(keep, a_wide[site, pl.ds(t, tile, stride=4), :], 0.0)
        am[site, t] = value.astype(jnp.bfloat16)
        at[site, t] = value.T.astype(jnp.bfloat16)

    def corner(side, site, s, t):
        value = m_wide[site, pl.ds(4 * s + t, padded, stride=16), :]
        if side == 0:
            full = jnp.concatenate(
                [value, jnp.zeros((tile - padded, tile), jnp.float32)], axis=0
            )
            value = full.T[:padded]
        return value

    def prepare_mpo(side, site, n):
        lo, hi = groups[n]
        for t in range(lo, hi):
            value = corner(side, site, lo, t)
            for s in range(lo + 1, hi):
                value = value + pltpu.roll(
                    corner(side, site, s, t), (s - lo) * padded, 1
                )
            value = value.astype(jnp.bfloat16)
            if n == 1:
                m_two[side, site, (t - lo) * padded : (t - lo + 1) * padded] = value
            else:
                m_one[side, site, n // 2] = value

    def mpo_of(side, site, n):
        if n == 1:
            return m_two[side, site, :, : 2 * padded]
        return m_one[side, site, n // 2, :, :padded]

    def stack_of(mats, site, n):
        lo, hi = groups[n]
        return mats[site, lo:hi].reshape((hi - lo) * tile, tile)

    one = functools.partial(stage_one, tile, padded, pitch)
    two = functools.partial(stage_two, tile, padded, pitch)
    every = (0, width)
    whole = (0, tile)

    def tall(c):
        return (c * rows, rows)

    def wide(c):
        return (c * SPAN, SPAN)

    def first(side, src, site, n, part, dst):
        one(*part, src, stack_of(am if side else at, site, n), dst)

    def second(side, site, n, part, src, acc, add):
        two(
            *part, src, mpo_of(side, site, n),
            stack_of(at if side else am, site, n), acc, add,
        )

    def both(side, src, site, n, acc, add):
        first(side, src, site, n, every, mid)
        second(side, site, n, whole, mid, acc, add)

    def ket(side, src, site, part):
        ket_first(
            width, padded, pitch, *part, src, stack_of(at if side else am, site, 2),
            mpo_of(side, site, 2), mid_ket, inner,
        )

    def bra(side, site, part, acc, dst):
        bra_last(
            tile, pitch, *part, inner, stack_of(am if side else at, site, 2), acc, dst
        )

    zero = jnp.zeros((tile, tile), jnp.float32)
    for w in range(width, padded):
        for buffer, s in ((mid, 0), (mid, 1), (mid_bra, 0), (mid_ket, 0)):
            buffer[pl.ds((s * padded + w) * pitch, tile), :] = zero
    m_wide[...] = jnp.zeros_like(m_wide)
    loads[0].wait()
    loads[1].wait()
    widen(0)
    prepare_tensor(0, 3)
    prepare_mpo(0, 0, 2)
    loads[2].wait()
    first(0, lin, 0, 2, every, mid)
    pl.semaphore_wait(barrier, 4)
    r_own = pieces("bond", rin_hbm, r_one.at[0], 0, {"sector": down})
    for copy in r_own:
        copy.start()
    p_own = pieces("bra", p_send.at[0], p_recv.at[0], 1, {"sector": up})
    for c in range(SLICES):
        second(0, 0, 2, tall(c), mid, acc_one, False)
        emit(pitch, every, tall(c), acc_one, None, p_send.at[0])
        p_own[c].start()
    for t in range(3):
        prepare_tensor(0, t)
    widen(1)
    for t in range(4):
        prepare_tensor(1, t)
    for side in range(2):
        for site in range(sites):
            for n in range(3):
                if (side, site, n) != (0, 0, 2):
                    prepare_mpo(side, site, n)

    both(0, lin, 0, 1, acc_one, False)
    loads[3].wait()
    both(1, rin, 1, 0, acc_right, False)
    s_own = pieces("bra", s_send.at[0], s_recv.at[0], 2, {"sector": up})
    r_pass = pieces("bond", r_one.at[0], r_two.at[0], 3, {"sector": down})

    def on_partial(c):
        p_own[c].wait_recv()
        emit(pitch, every, tall(c), acc_one, p_recv.at[0], s_send.at[0])
        s_own[c].start()

    def on_right(c):
        r_own[c].wait_recv()
        r_pass[c].start()

    in_order((chunks, on_right), (SLICES, on_partial))
    both(0, lin, 0, 0, acc_zero, False)
    both(1, r_one.at[0], 1, 1, acc_right, True)

    def on_sum(c):
        s_own[c].wait_recv()
        emit(pitch, every, tall(c), acc_zero, s_recv.at[0], left_out.at[0])
        ket(0, left_out.at[0], 1, tall(c))

    def on_second_right(c):
        r_pass[c].wait_recv()
        first(1, r_two.at[0], 1, 2, wide(c), mid_bra)

    in_order((chunks, on_second_right), (SLICES, on_sum))
    copies = r_own + p_own + s_own + r_pass

    p_own = pieces("bond", p_send.at[1], p_recv.at[1], 5, {"sector": up})
    r_own = pieces("bra", right_out.at[1], r_one.at[1], 4, {"sector": down})

    def send_partial(c):
        bra(0, 1, wide(c), None, p_send.at[1])
        p_own[c].start()

    def send_right(c):
        second(1, 1, 2, tall(c), mid_bra, acc_right, True)
        emit(pitch, every, tall(c), acc_right, None, right_out.at[1])
        r_own[c].start()

    in_order((chunks, send_partial), (SLICES, send_right))

    both(0, left_out.at[0], 1, 1, acc_one, False)
    both(1, right_out.at[1], 0, 0, acc_right, False)
    s_own = pieces("bond", s_send.at[1], s_recv.at[1], 6, {"sector": up})
    r_pass = pieces("bra", r_one.at[1], r_two.at[1], 7, {"sector": down})
    edges = pieces("bond", left_out.at[1], edge_out, 8, {"chain": after})

    def on_partial(c):
        p_own[c].wait_recv()
        emit(pitch, wide(c), whole, acc_one, p_recv.at[1], s_send.at[1])
        s_own[c].start()

    def on_right(c):
        r_own[c].wait_recv()
        r_pass[c].start()

    in_order((SLICES, on_right), (chunks, on_partial))
    both(0, left_out.at[0], 1, 0, acc_zero, False)
    both(1, r_one.at[1], 0, 1, acc_right, True)

    def on_sum(c):
        s_own[c].wait_recv()
        emit(pitch, wide(c), whole, acc_zero, s_recv.at[1], left_out.at[1])

        @pl.when(chain < chain_count - 1)
        def _():
            edges[c].start()

    def on_second_right(c):
        r_pass[c].wait_recv()
        ket(1, r_two.at[1], 0, tall(c))

    in_order((chunks, on_sum), (SLICES, on_second_right))
    bra(1, 0, every, acc_right, right_out.at[0])
    copies += r_own + p_own + s_own + r_pass

    @pl.when(chain == 0)
    def _():
        keep_edge.wait()

    @pl.when(chain > 0)
    def _():
        for edge in edges:
            edge.wait_recv()

    @pl.when(chain < chain_count - 1)
    def _():
        for edge in edges:
            edge.wait_send()

    for copy in copies:
        copy.wait_send()


def shards(chain_count, sector_count, site_tensors, mpo, left_in, right_in, tile_rows):
    sites, _, tile, phys, _ = site_tensors.shape
    width = mpo.shape[1]
    padded = -(-width // 16) * 16
    pitch = tile + PITCH_EXTRA
    tensors = site_tensors.reshape(sites, tile * phys, tile)
    flat_mpo = mpo.transpose(0, 1, 3, 4, 2).reshape(sites, width * 16, width)
    env = (width, tile, tile)
    sizes = (chain_count, sector_count, sites, width, tile, padded, pitch)
    vmem = pl.BlockSpec(memory_space=pltpu.VMEM)
    hbm = pl.BlockSpec(memory_space=pl.ANY)
    streams = 4 * sites + 1
    most = max(SLICES, width // SPAN)
    left, right, edge = pl.pallas_call(
        functools.partial(kernel, sizes),
        out_shape=(
            pltpu.VMEM((sites,) + env, jnp.bfloat16),
            pltpu.VMEM((sites,) + env, jnp.bfloat16),
            pltpu.VMEM(env, jnp.bfloat16),
        ),
        in_specs=[pl.BlockSpec(memory_space=pltpu.SMEM)] + [hbm] * 4,
        out_specs=[vmem] * 3,
        scratch_shapes=[pltpu.VMEM(env, jnp.bfloat16)] * 2
        + [pltpu.VMEM((sites,) + env, jnp.bfloat16)] * 6
        + [
            pltpu.VMEM((2 * padded * pitch, tile), jnp.float32),
        ]
        + [pltpu.VMEM((padded * pitch, tile), jnp.float32)] * 6
        + [
            pltpu.VMEM((sites, phys, tile, tile), jnp.bfloat16),
            pltpu.VMEM((sites, phys, tile, tile), jnp.bfloat16),
            pltpu.VMEM((2, sites, 2, padded, tile), jnp.bfloat16),
            pltpu.VMEM((2, sites, 2 * padded, tile), jnp.bfloat16),
            pltpu.VMEM((sites, phys * tile, tile), jnp.bfloat16),
            pltpu.VMEM((sites, 16 * width, width), jnp.bfloat16),
            pltpu.VMEM((sites, phys * tile, tile), jnp.float32),
            pltpu.VMEM((sites, 16 * padded, tile), jnp.float32),
            pltpu.SemaphoreType.DMA((streams, most)),
            pltpu.SemaphoreType.DMA((streams, most)),
            pltpu.SemaphoreType.DMA((5,)),
        ],
        compiler_params=pltpu.CompilerParams(
            collective_id=0, has_side_effects=True, vmem_limit_bytes=52 << 20
        ),
    )(tile_rows, tensors, flat_mpo, left_in[0, 0], right_in[0, 0])
    return left[:, None], right[:, None], edge[None, None]


def solution(mesh):
    envs = P("chain", "sector", None, None, None)
    return jax.shard_map(
        functools.partial(shards, mesh.shape["chain"], mesh.shape["sector"]),
        mesh=mesh,
        in_specs=(envs, P("chain", None, None, None, None), envs, envs, P()),
        out_specs=(envs, envs, envs),
        check_vma=False,
    )
```

```python
import functools

import jax
import jax.numpy as jnp
from jax import lax
from jax.experimental import pallas as pl
from jax.experimental.pallas import tpu as pltpu
from jax.sharding import PartitionSpec as P

groups = ((0, 1), (1, 3), (3, 4))
charge = (0, 1, 1, 2)
SLICES = 8
SPAN = 6
ENDS = (4, 2)
PITCH_EXTRA = 8
ROWS = 16
PAIRS = 3


def stage_one(tile, padded, pitch, start, width, src, lhs, mid):
    count = lhs.shape[0] // tile
    pairs = width // 2
    unroll = max(n for n in range(1, PAIRS + 1) if pairs % n == 0)

    def body(i, carry):
        for k in range(unroll):
            w = start + (i * unroll + k) * 2
            rhs = jnp.concatenate([src[w], src[w + 1]], axis=1)
            prod = jnp.dot(lhs, rhs, preferred_element_type=jnp.float32)
            for s in range(count):
                for j in range(2):
                    row = pl.multiple_of((s * padded + w + j) * pitch, 8)
                    mid[pl.ds(row, tile), :] = prod[
                        s * tile : (s + 1) * tile, j * tile : (j + 1) * tile
                    ]
        return carry

    lax.fori_loop(0, pairs // unroll, body, 0)


def stage_two(tile, padded, pitch, start, rows, mid, mpo_part, fin, out, add):
    count = fin.shape[0] // tile

    def block(i, carry):
        base = start + i * ROWS
        left = []
        for j in range(0, ROWS, 2):
            both = [
                mid[pl.ds(base + j + k, count * padded, stride=pitch), :].astype(
                    jnp.bfloat16
                )
                for k in range(2)
            ]
            inner = jnp.dot(
                mpo_part,
                jnp.concatenate(both, axis=1),
                preferred_element_type=jnp.float32,
            ).astype(jnp.bfloat16)
            for k in range(2):
                left.append(
                    jnp.concatenate(
                        [
                            inner[
                                t * padded : (t + 1) * padded,
                                k * tile : (k + 1) * tile,
                            ]
                            for t in range(count)
                        ],
                        axis=1,
                    )
                )
        prod = jnp.dot(
            jnp.concatenate(left, axis=0), fin, preferred_element_type=jnp.float32
        )
        for j in range(ROWS):
            spot = pl.ds(base + j, padded, stride=pitch)
            value = prod[j * padded : (j + 1) * padded]
            if add:
                value = value + out[spot, :]
            out[spot, :] = value
        return carry

    lax.fori_loop(0, rows // ROWS, block, 0)


def ket_first(width, padded, pitch, start, rows, src, fin, mpo_part, mid, inner):
    group = max(n for n in range(1, 22) if width % n == 0)

    def body(i, carry):
        first = i * group
        block = src[pl.ds(first, group), start : start + rows, :]
        prod = jnp.dot(
            block.reshape(group * rows, block.shape[2]),
            fin,
            preferred_element_type=jnp.float32,
        )
        for k in range(group):
            row = pl.multiple_of((first + k) * pitch + start, 8)
            mid[pl.ds(row, rows), :] = prod[k * rows : (k + 1) * rows]
        return carry

    lax.fori_loop(0, width // group, body, 0)
    tile = fin.shape[1]

    def block(i, carry):
        for j in range(0, ROWS, 2):
            base = start + i * ROWS + j
            both = [
                mid[pl.ds(base + k, padded, stride=pitch), :].astype(jnp.bfloat16)
                for k in range(2)
            ]
            prod = jnp.dot(
                mpo_part,
                jnp.concatenate(both, axis=1),
                preferred_element_type=jnp.float32,
            )
            for k in range(2):
                inner[pl.ds(base + k, padded, stride=pitch), :] = prod[
                    :, k * tile : (k + 1) * tile
                ]
        return carry

    lax.fori_loop(0, rows // ROWS, block, 0)


def bra_last(tile, pitch, start, width, inner, lhs, acc, dst):
    for w in range(start, start + width, 2):
        rows = [pl.ds((w + k) * pitch, tile) for k in range(2)]
        rhs = jnp.concatenate(
            [inner[row, :].astype(jnp.bfloat16) for row in rows], axis=1
        )
        prod = jnp.dot(lhs, rhs, preferred_element_type=jnp.float32)
        for k in range(2):
            value = prod[:, k * tile : (k + 1) * tile]
            if acc is not None:
                value = value + acc[rows[k], :]
            dst[w + k] = value.astype(jnp.bfloat16)


def emit(pitch, wide, tall, acc, other, dst):
    first, width = wide
    start, rows = tall

    def one(i, carry):
        for k in range(2):
            w = first + 2 * i + k
            value = acc[pl.ds(pl.multiple_of(w * pitch + start, 8), rows), :]
            if other is not None:
                value = value + other[w, start : start + rows, :].astype(jnp.float32)
            dst[w, start : start + rows, :] = value.astype(jnp.bfloat16)
        return carry

    lax.fori_loop(0, width // 2, one, 0)


def chunks_of(width):
    spans = [SPAN] * ((width - sum(ENDS)) // SPAN)
    spans += [width - sum(ENDS) - sum(spans)] + list(ENDS)
    spans = [span for span in spans if span]
    return [(sum(spans[:i]), span) for i, span in enumerate(spans)]


def in_order(*lists):
    spots = []
    for at, (count, act) in enumerate(lists):
        spots += [((c + 1) / count, at, c, act) for c in range(count)]
    for _, _, c, act in sorted(spots, key=lambda spot: spot[:3]):
        act(c)


def kernel(
    sizes,
    rows_hbm, a_hbm, m_hbm, lin_hbm, rin_hbm,
    left_out, right_out, edge_out,
    lin, rin, r_one, r_two, p_send, p_recv, s_send, s_recv,
    mid, mid_bra, mid_ket, inner, acc_one, acc_zero, acc_right,
    am, at, m_one, m_two, a_in, m_in, a_wide, m_wide, rows_ref,
    send_sem, recv_sem, load_sem,
):
    chain_count, sector_count, sites, width, tile, padded, pitch = sizes
    chain = lax.axis_index("chain")
    sector = lax.axis_index("sector")
    up = lax.rem(sector + 1, sector_count)
    down = lax.rem(sector + sector_count - 1, sector_count)
    after = lax.rem(chain + 1, chain_count)
    before = lax.rem(chain + chain_count - 1, chain_count)
    rows = tile // SLICES
    parts = chunks_of(width)
    chunks = len(parts)
    even = lax.rem(chain, 2) == 0

    barrier = pltpu.get_barrier_semaphore()
    for there in ({"sector": up}, {"sector": down}, {"chain": after}, {"chain": before}):
        pl.semaphore_signal(barrier, inc=1, device_id=there)
    loads = [
        pltpu.make_async_copy(src, dst, load_sem.at[i])
        for i, (src, dst) in enumerate(
            ((rows_hbm, rows_ref), (a_hbm, a_in), (m_hbm, m_in), (lin_hbm, lin), (rin_hbm, rin))
        )
    ]
    for load in loads:
        load.start()
    keep_edge = pltpu.make_async_copy(lin_hbm, edge_out, load_sem.at[5])

    @pl.when(chain == 0)
    def _():
        keep_edge.start()

    def piece(form, src, dst, stream, c, there):
        if form == "bra":
            cut = (slice(None), pl.ds(c * rows, rows), slice(None))
        else:
            cut = (pl.ds(*parts[c]), slice(None), slice(None))
        return pltpu.make_async_remote_copy(
            src_ref=src.at[cut],
            dst_ref=dst.at[cut],
            send_sem=send_sem.at[stream, c],
            recv_sem=recv_sem.at[stream, c],
            device_id=there,
            device_id_type=pl.DeviceIdType.MESH,
        )

    def pieces(form, src, dst, stream, there):
        count = SLICES if form == "bra" else chunks
        return [piece(form, src, dst, stream, c, there) for c in range(count)]

    ids_a = lax.broadcasted_iota(jnp.int32, (tile, tile), 0)
    ids_b = lax.broadcasted_iota(jnp.int32, (tile, tile), 1)

    def widen(site):
        a_wide[site] = a_in[site].astype(jnp.float32)
        m_wide[site, 0 : 16 * width, 0:width] = m_in[site].astype(jnp.float32)

    def prepare_tensor(site, t):
        bond = chain * sites + site
        there = sector + charge[t]
        seen = rows_ref[bond + 1, jnp.minimum(there, sector_count - 1)]
        high = jnp.where(there < sector_count, seen, 0)
        keep = (ids_a < rows_ref[bond, sector]) & (ids_b < high)
        value = jnp.where(keep, a_wide[site, pl.ds(t, tile, stride=4), :], 0.0)
        am[site, t] = value.astype(jnp.bfloat16)
        at[site, t] = value.T.astype(jnp.bfloat16)

    def corner(side, site, s, t):
        value = m_wide[site, pl.ds(4 * s + t, padded, stride=16), :]
        if side == 0:
            full = jnp.concatenate(
                [value, jnp.zeros((tile - padded, tile), jnp.float32)], axis=0
            )
            value = full.T[:padded]
        return value

    def prepare_mpo(side, site, n):
        lo, hi = groups[n]
        for t in range(lo, hi):
            value = corner(side, site, lo, t)
            for s in range(lo + 1, hi):
                value = value + pltpu.roll(
                    corner(side, site, s, t), (s - lo) * padded, 1
                )
            value = value.astype(jnp.bfloat16)
            if n == 1:
                m_two[side, site, (t - lo) * padded : (t - lo + 1) * padded] = value
            else:
                m_one[side, site, n // 2] = value

    def mpo_of(side, site, n):
        if n == 1:
            return m_two[side, site, :, : 2 * padded]
        return m_one[side, site, n // 2, :, :padded]

    def stack_of(mats, site, n):
        lo, hi = groups[n]
        return mats[site, lo:hi].reshape((hi - lo) * tile, tile)

    one = functools.partial(stage_one, tile, padded, pitch)
    two = functools.partial(stage_two, tile, padded, pitch)
    every = (0, width)
    whole = (0, tile)

    def tall(c):
        return (c * rows, rows)

    def wide(c):
        return parts[c]

    def first(side, src, site, n, part, dst):
        one(*part, src, stack_of(am if side else at, site, n), dst)

    def second(side, site, n, part, src, acc, add):
        two(
            *part, src, mpo_of(side, site, n),
            stack_of(at if side else am, site, n), acc, add,
        )

    def both(side, src, site, n, acc, add):
        first(side, src, site, n, every, mid)
        second(side, site, n, whole, mid, acc, add)

    def ket(side, src, site, part):
        ket_first(
            width, padded, pitch, *part, src, stack_of(at if side else am, site, 2),
            mpo_of(side, site, 2), mid_ket, inner,
        )

    def bra(side, site, part, acc, dst):
        bra_last(
            tile, pitch, *part, inner, stack_of(am if side else at, site, 2), acc, dst
        )

    m_wide[...] = jnp.zeros_like(m_wide)
    zero = jnp.zeros((tile, tile), jnp.float32)
    for w in range(width, padded):
        for buffer, s in ((mid, 0), (mid, 1), (mid_bra, 0), (mid_ket, 0)):
            buffer[pl.ds((s * padded + w) * pitch, tile), :] = zero
    for i in range(3):
        loads[i].wait()
    widen(0)
    prepare_tensor(0, 3)
    prepare_mpo(0, 0, 2)
    loads[3].wait()
    first(0, lin, 0, 2, every, mid)
    pl.semaphore_wait(barrier, 4)
    r_own = pieces("bond", rin_hbm, r_one.at[0], 0, {"sector": down})
    p_own = pieces("bra", p_send.at[0], p_recv.at[0], 1, {"sector": up})

    @pl.when(even)
    def _():
        for copy in r_own:
            copy.start()

    for c in range(SLICES):
        second(0, 0, 2, tall(c), mid, acc_one, False)
        emit(pitch, every, tall(c), acc_one, None, p_send.at[0])
        pl.when(even)(p_own[c].start)
    for t in range(3):
        prepare_tensor(0, t)
    widen(1)
    for t in range(4):
        prepare_tensor(1, t)
    for side in range(2):
        for site in range(sites):
            for n in range(3):
                if (side, site, n) != (0, 0, 2):
                    prepare_mpo(side, site, n)

    both(0, lin, 0, 1, acc_one, False)
    loads[4].wait()
    both(1, rin, 1, 0, acc_right, False)

    @pl.when(jnp.logical_not(even))
    def _():
        for copy in r_own + p_own:
            copy.start()

    s_own = pieces("bra", s_send.at[0], s_recv.at[0], 2, {"sector": up})
    r_pass = pieces("bond", r_one.at[0], r_two.at[0], 3, {"sector": down})

    def on_partial(c):
        p_own[c].wait_recv()
        emit(pitch, every, tall(c), acc_one, p_recv.at[0], s_send.at[0])
        s_own[c].start()

    def on_right(c):
        r_own[c].wait_recv()
        r_pass[c].start()

    in_order((chunks, on_right), (SLICES, on_partial))
    both(0, lin, 0, 0, acc_zero, False)
    both(1, r_one.at[0], 1, 1, acc_right, True)

    def on_sum(c):
        s_own[c].wait_recv()
        emit(pitch, every, tall(c), acc_zero, s_recv.at[0], left_out.at[0])
        ket(0, left_out.at[0], 1, tall(c))

    def on_second_right(c):
        r_pass[c].wait_recv()
        first(1, r_two.at[0], 1, 2, wide(c), mid_bra)

    in_order((chunks, on_second_right), (SLICES, on_sum))
    copies = r_own + p_own + s_own + r_pass

    p_own = pieces("bond", p_send.at[1], p_recv.at[1], 5, {"sector": up})
    r_own = pieces("bra", right_out.at[1], r_one.at[1], 4, {"sector": down})

    def send_partial(c):
        bra(0, 1, wide(c), None, p_send.at[1])
        p_own[c].start()

    def send_right(c):
        second(1, 1, 2, tall(c), mid_bra, acc_right, True)
        emit(pitch, every, tall(c), acc_right, None, right_out.at[1])
        r_own[c].start()

    in_order((chunks, send_partial), (SLICES, send_right))

    both(0, left_out.at[0], 1, 1, acc_one, False)
    both(1, right_out.at[1], 0, 0, acc_right, False)
    s_own = pieces("bond", s_send.at[1], s_recv.at[1], 6, {"sector": up})
    r_pass = pieces("bra", r_one.at[1], r_two.at[1], 7, {"sector": down})
    edges = pieces("bond", left_out.at[1], edge_out, 8, {"chain": after})

    def on_partial(c):
        p_own[c].wait_recv()
        emit(pitch, wide(c), whole, acc_one, p_recv.at[1], s_send.at[1])
        s_own[c].start()

    def on_right(c):
        r_own[c].wait_recv()
        r_pass[c].start()

    in_order((SLICES, on_right), (chunks, on_partial))
    both(0, left_out.at[0], 1, 0, acc_zero, False)

    def on_sum(c):
        s_own[c].wait_recv()
        emit(pitch, wide(c), whole, acc_zero, s_recv.at[1], left_out.at[1])

        @pl.when(chain < chain_count - 1)
        def _():
            edges[c].start()

    def on_second_right(c):
        r_pass[c].wait_recv()
        ket(1, r_two.at[1], 0, tall(c))

    on_sum(0)
    on_sum(1)
    first(1, r_one.at[1], 0, 1, every, mid)
    on_sum(2)
    quarters = [(i * tile // 4, tile // 4) for i in range(4)]
    for i in range(2):
        second(1, 0, 1, quarters[i], mid, acc_right, True)
    on_sum(3)
    for i in range(2, 4):
        second(1, 0, 1, quarters[i], mid, acc_right, True)
    in_order((chunks - 4, lambda c: on_sum(c + 4)), (SLICES, on_second_right))
    bra(1, 0, every, acc_right, right_out.at[0])
    copies += r_own + p_own + s_own + r_pass

    @pl.when(chain == 0)
    def _():
        keep_edge.wait()

    @pl.when(chain > 0)
    def _():
        for edge in edges:
            edge.wait_recv()

    @pl.when(chain < chain_count - 1)
    def _():
        for edge in edges:
            edge.wait_send()

    for copy in copies:
        copy.wait_send()


def leave(left, right, edge):
    def body(left, right, edge, left_out, right_out, edge_out, sem):
        pairs = [(edge, edge_out.at[0, 0])]
        for src, dst in ((left, left_out), (right, right_out)):
            pairs += [(src.at[i], dst.at[i, 0]) for i in range(src.shape[0])]
        copies = [
            pltpu.make_async_copy(src, dst, sem.at[i])
            for i, (src, dst) in enumerate(pairs)
        ]
        for copy in copies:
            copy.start()
        for copy in copies:
            copy.wait()

    env = edge.shape
    sites = left.shape[0]
    hbm = pl.BlockSpec(memory_space=pl.ANY)
    return pl.pallas_call(
        body,
        out_shape=(
            jax.ShapeDtypeStruct((sites, 1) + env, left.dtype),
            jax.ShapeDtypeStruct((sites, 1) + env, left.dtype),
            jax.ShapeDtypeStruct((1, 1) + env, left.dtype),
        ),
        in_specs=[pl.BlockSpec(memory_space=pltpu.VMEM)] * 3,
        out_specs=[hbm] * 3,
        scratch_shapes=[pltpu.SemaphoreType.DMA((2 * sites + 1,))],
        compiler_params=pltpu.CompilerParams(vmem_limit_bytes=16 << 20),
    )(left, right, edge)


def shards(chain_count, sector_count, site_tensors, mpo, left_in, right_in, tile_rows):
    sites, _, tile, phys, _ = site_tensors.shape
    width = mpo.shape[1]
    padded = -(-width // 16) * 16
    pitch = tile + PITCH_EXTRA
    tensors = site_tensors.reshape(sites, tile * phys, tile)
    flat_mpo = mpo.transpose(0, 1, 3, 4, 2).reshape(sites, width * 16, width)
    env = (width, tile, tile)
    sizes = (chain_count, sector_count, sites, width, tile, padded, pitch)
    vmem = pl.BlockSpec(memory_space=pltpu.VMEM)
    hbm = pl.BlockSpec(memory_space=pl.ANY)
    streams = 4 * sites + 1
    most = max(SLICES, len(chunks_of(width)))
    left, right, edge = pl.pallas_call(
        functools.partial(kernel, sizes),
        out_shape=(
            pltpu.VMEM((sites,) + env, jnp.bfloat16),
            pltpu.VMEM((sites,) + env, jnp.bfloat16),
            pltpu.VMEM(env, jnp.bfloat16),
        ),
        in_specs=[hbm] * 5,
        out_specs=[vmem] * 3,
        scratch_shapes=[pltpu.VMEM(env, jnp.bfloat16)] * 2
        + [pltpu.VMEM((sites,) + env, jnp.bfloat16)] * 6
        + [
            pltpu.VMEM((2 * padded * pitch, tile), jnp.float32),
        ]
        + [pltpu.VMEM((padded * pitch, tile), jnp.float32)] * 6
        + [
            pltpu.VMEM((sites, phys, tile, tile), jnp.bfloat16),
            pltpu.VMEM((sites, phys, tile, tile), jnp.bfloat16),
            pltpu.VMEM((2, sites, 2, padded, tile), jnp.bfloat16),
            pltpu.VMEM((2, sites, 2 * padded, tile), jnp.bfloat16),
            pltpu.VMEM((sites, phys * tile, tile), jnp.bfloat16),
            pltpu.VMEM((sites, 16 * width, width), jnp.bfloat16),
            pltpu.VMEM((sites, phys * tile, tile), jnp.float32),
            pltpu.VMEM((sites, 16 * padded, tile), jnp.float32),
            pltpu.SMEM(tile_rows.shape, tile_rows.dtype),
            pltpu.SemaphoreType.DMA((streams, most)),
            pltpu.SemaphoreType.DMA((streams, most)),
            pltpu.SemaphoreType.DMA((6,)),
        ],
        compiler_params=pltpu.CompilerParams(
            collective_id=0, has_side_effects=True, vmem_limit_bytes=52 << 20
        ),
    )(tile_rows, tensors, flat_mpo, left_in[0, 0], right_in[0, 0])
    return leave(left, right, edge)


def solution(mesh):
    envs = P("chain", "sector", None, None, None)
    return jax.shard_map(
        functools.partial(shards, mesh.shape["chain"], mesh.shape["sector"]),
        mesh=mesh,
        in_specs=(envs, P("chain", None, None, None, None), envs, envs, P()),
        out_specs=(envs, envs, envs),
        check_vma=False,
    )
```

```python
import functools

import jax
import jax.numpy as jnp
from jax import lax
from jax.experimental import pallas as pl
from jax.experimental.pallas import tpu as pltpu
from jax.sharding import PartitionSpec as P

groups = ((0, 1), (1, 3), (3, 4))
charge = (0, 1, 1, 2)
SLICES = 8
SPAN = 6
ENDS = (2, 4)
PITCH_EXTRA = 8
PARTS = 3
ROWS = 16
PAIRS = 3


def stage_one(tile, padded, pitch, start, width, src, lhs, mid):
    count = lhs.shape[0] // tile
    pairs = width // 2
    unroll = max(n for n in range(1, PAIRS + 1) if pairs % n == 0)

    def body(i, carry):
        for k in range(unroll):
            w = start + (i * unroll + k) * 2
            rhs = jnp.concatenate([src[w], src[w + 1]], axis=1)
            prod = jnp.dot(lhs, rhs, preferred_element_type=jnp.float32)
            for s in range(count):
                for j in range(2):
                    row = pl.multiple_of((s * padded + w + j) * pitch, 8)
                    mid[pl.ds(row, tile), :] = prod[
                        s * tile : (s + 1) * tile, j * tile : (j + 1) * tile
                    ]
        return carry

    lax.fori_loop(0, pairs // unroll, body, 0)


def stage_two(tile, padded, pitch, start, rows, mid, mpo_part, fin, out, add):
    count = fin.shape[0] // tile

    def block(i, carry):
        base = start + i * ROWS
        left = []
        for j in range(0, ROWS, 2):
            both = [
                mid[pl.ds(base + j + k, count * padded, stride=pitch), :].astype(
                    jnp.bfloat16
                )
                for k in range(2)
            ]
            inner = jnp.dot(
                mpo_part,
                jnp.concatenate(both, axis=1),
                preferred_element_type=jnp.float32,
            ).astype(jnp.bfloat16)
            for k in range(2):
                left.append(
                    jnp.concatenate(
                        [
                            inner[
                                t * padded : (t + 1) * padded,
                                k * tile : (k + 1) * tile,
                            ]
                            for t in range(count)
                        ],
                        axis=1,
                    )
                )
        prod = jnp.dot(
            jnp.concatenate(left, axis=0), fin, preferred_element_type=jnp.float32
        )
        for j in range(ROWS):
            spot = pl.ds(base + j, padded, stride=pitch)
            value = prod[j * padded : (j + 1) * padded]
            if add:
                value = value + out[spot, :]
            out[spot, :] = value
        return carry

    lax.fori_loop(0, rows // ROWS, block, 0)


def ket_first(width, padded, pitch, start, rows, src, fin, mpo_part, mid, inner):
    group = max(n for n in range(1, 22) if width % n == 0)

    def body(i, carry):
        first = i * group
        block = src[pl.ds(first, group), start : start + rows, :]
        prod = jnp.dot(
            block.reshape(group * rows, block.shape[2]),
            fin,
            preferred_element_type=jnp.float32,
        )
        for k in range(group):
            row = pl.multiple_of((first + k) * pitch + start, 8)
            mid[pl.ds(row, rows), :] = prod[k * rows : (k + 1) * rows]
        return carry

    lax.fori_loop(0, width // group, body, 0)
    tile = fin.shape[1]

    def block(i, carry):
        for j in range(0, ROWS, 2):
            base = start + i * ROWS + j
            both = [
                mid[pl.ds(base + k, padded, stride=pitch), :].astype(jnp.bfloat16)
                for k in range(2)
            ]
            prod = jnp.dot(
                mpo_part,
                jnp.concatenate(both, axis=1),
                preferred_element_type=jnp.float32,
            )
            for k in range(2):
                inner[pl.ds(base + k, padded, stride=pitch), :] = prod[
                    :, k * tile : (k + 1) * tile
                ]
        return carry

    lax.fori_loop(0, rows // ROWS, block, 0)


def bra_last(tile, pitch, start, width, inner, lhs, acc, dst):
    for w in range(start, start + width, 2):
        rows = [pl.ds((w + k) * pitch, tile) for k in range(2)]
        rhs = jnp.concatenate(
            [inner[row, :].astype(jnp.bfloat16) for row in rows], axis=1
        )
        prod = jnp.dot(lhs, rhs, preferred_element_type=jnp.float32)
        for k in range(2):
            value = prod[:, k * tile : (k + 1) * tile]
            if acc is not None:
                value = value + acc[rows[k], :]
            dst[w + k] = value.astype(jnp.bfloat16)


def emit(pitch, wide, tall, acc, other, dst):
    first, width = wide
    start, rows = tall

    def one(i, carry):
        for k in range(2):
            w = first + 2 * i + k
            value = acc[pl.ds(pl.multiple_of(w * pitch + start, 8), rows), :]
            if other is not None:
                value = value + other[w, start : start + rows, :].astype(jnp.float32)
            dst[w, start : start + rows, :] = value.astype(jnp.bfloat16)
        return carry

    lax.fori_loop(0, width // 2, one, 0)


def chunks_of(width):
    middle = width - 2 * sum(ENDS)
    spans = list(ENDS) + [SPAN] * (middle // SPAN) + [middle % SPAN] + list(ENDS[::-1])
    spans = [span for span in spans if span]
    return [(sum(spans[:i]), span) for i, span in enumerate(spans)]


def in_order(*lists):
    spots = []
    for at, (ends, act) in enumerate(lists):
        spots += [(end, at, c, act) for c, end in enumerate(ends)]
    for _, _, c, act in sorted(spots, key=lambda spot: spot[:3]):
        act(c)


class Stream:
    def __init__(self, copies, send, receive):
        self.copies, self.send, self.receive = copies, send, receive

    def start(self, c, also=None):
        send = self.send if also is None else jnp.logical_and(self.send, also)
        pl.when(send)(self.copies[c].start)

    def start_all(self, also):
        @pl.when(jnp.logical_and(self.send, also))
        def _():
            for copy in self.copies:
                copy.start()

    def wait_recv(self, c):
        pl.when(self.receive)(self.copies[c].wait_recv)

    def wait_all(self):
        @pl.when(self.receive)
        def _():
            for copy in self.copies:
                copy.wait_recv()

    def finish(self):
        @pl.when(self.send)
        def _():
            for copy in self.copies:
                copy.wait_send()


def kernel(
    sizes,
    rows_hbm, a_hbm, m_hbm, lin_hbm, rin_hbm,
    left_out, right_out, edge_out,
    lin, rin, r_one, r_two, p_send, p_recv, s_send, s_recv,
    mid, mid_bra, mid_ket, inner, acc_one, acc_zero, acc_right,
    am, at, m_one, m_two, a_in, m_in, a_wide, m_wide, rows_ref,
    send_sem, recv_sem, load_sem,
):
    chain_count, sector_count, sites, width, tile, padded, pitch = sizes
    chain = lax.axis_index("chain")
    sector = lax.axis_index("sector")
    up = lax.rem(sector + 1, sector_count)
    down = lax.rem(sector + sector_count - 1, sector_count)
    after = lax.rem(chain + 1, chain_count)
    before = lax.rem(chain + chain_count - 1, chain_count)
    rows = tile // SLICES
    parts = chunks_of(width)
    chunks = len(parts)
    ahead = lax.rem(chain, 2) == 1
    bra_ends = [(c + 1) / SLICES for c in range(SLICES)]
    bond_ends = [sum(part) / width for part in parts]
    above, below = sector < sector_count - 1, sector > 0
    later, earlier = chain < chain_count - 1, chain > 0

    barrier = pltpu.get_barrier_semaphore()
    greeted = jnp.int32(0)
    for known, there in (
        (above, {"sector": up}),
        (below, {"sector": down}),
        (later, {"chain": after}),
        (earlier, {"chain": before}),
    ):

        @pl.when(known)
        def _(there=there):
            pl.semaphore_signal(barrier, inc=1, device_id=there)

        greeted = greeted + jnp.where(known, 1, 0)
    loads = [
        pltpu.make_async_copy(src, dst, load_sem.at[i])
        for i, (src, dst) in enumerate(
            ((rows_hbm, rows_ref), (a_hbm, a_in), (m_hbm, m_in), (lin_hbm, lin), (rin_hbm, rin))
        )
    ]
    for load in loads:
        load.start()
    keep_edge = pltpu.make_async_copy(lin_hbm, edge_out, load_sem.at[5])

    @pl.when(chain == 0)
    def _():
        keep_edge.start()

    def piece(form, src, dst, stream, c, there):
        if form == "bra":
            cut = (slice(None), pl.ds(c * rows, rows), slice(None))
        else:
            cut = (pl.ds(*parts[c]), slice(None), slice(None))
        return pltpu.make_async_remote_copy(
            src_ref=src.at[cut],
            dst_ref=dst.at[cut],
            send_sem=send_sem.at[stream, c],
            recv_sem=recv_sem.at[stream, c],
            device_id=there,
            device_id_type=pl.DeviceIdType.MESH,
        )

    def pieces(form, src, dst, stream, there):
        count = SLICES if form == "bra" else chunks
        copies = [piece(form, src, dst, stream, c, there) for c in range(count)]
        send, receive = {
            0: (below, above),
            1: (above, below),
            2: (above, below),
            3: (below & above, sector < sector_count - 2),
        }[stream % 4]
        return Stream(copies, send, receive)

    ids_a = lax.broadcasted_iota(jnp.int32, (tile, tile), 0)
    ids_b = lax.broadcasted_iota(jnp.int32, (tile, tile), 1)

    def widen(site):
        a_wide[site] = a_in[site].astype(jnp.float32)
        m_wide[site, 0 : 16 * width, 0:width] = m_in[site].astype(jnp.float32)

    def prepare_tensor(site, t):
        bond = chain * sites + site
        there = sector + charge[t]
        seen = rows_ref[bond + 1, jnp.minimum(there, sector_count - 1)]
        high = jnp.where(there < sector_count, seen, 0)
        keep = (ids_a < rows_ref[bond, sector]) & (ids_b < high)
        value = jnp.where(keep, a_wide[site, pl.ds(t, tile, stride=4), :], 0.0)
        am[site, t] = value.astype(jnp.bfloat16)
        at[site, t] = value.T.astype(jnp.bfloat16)

    def corner(side, site, s, t):
        value = m_wide[site, pl.ds(4 * s + t, padded, stride=16), :]
        if side == 0:
            full = jnp.concatenate(
                [value, jnp.zeros((tile - padded, tile), jnp.float32)], axis=0
            )
            value = full.T[:padded]
        return value

    def prepare_mpo(side, site, n):
        lo, hi = groups[n]
        for t in range(lo, hi):
            value = corner(side, site, lo, t)
            for s in range(lo + 1, hi):
                value = value + pltpu.roll(
                    corner(side, site, s, t), (s - lo) * padded, 1
                )
            value = value.astype(jnp.bfloat16)
            if n == 1:
                m_two[side, site, (t - lo) * padded : (t - lo + 1) * padded] = value
            else:
                m_one[side, site, n // 2] = value

    def mpo_of(side, site, n):
        if n == 1:
            return m_two[side, site, :, : 2 * padded]
        return m_one[side, site, n // 2, :, :padded]

    def stack_of(mats, site, n):
        lo, hi = groups[n]
        return mats[site, lo:hi].reshape((hi - lo) * tile, tile)

    one = functools.partial(stage_one, tile, padded, pitch)
    two = functools.partial(stage_two, tile, padded, pitch)
    every = (0, width)
    whole = (0, tile)

    def tall(c):
        return (c * rows, rows)

    def wide(c):
        return parts[c]

    def first(side, src, site, n, part, dst):
        one(*part, src, stack_of(am if side else at, site, n), dst)

    def second(side, site, n, part, src, acc, add):
        two(
            *part, src, mpo_of(side, site, n),
            stack_of(at if side else am, site, n), acc, add,
        )

    def both(side, src, site, n, acc, add):
        first(side, src, site, n, every, mid)
        second(side, site, n, whole, mid, acc, add)

    def ket(side, src, site, part):
        ket_first(
            width, padded, pitch, *part, src, stack_of(at if side else am, site, 2),
            mpo_of(side, site, 2), mid_ket, inner,
        )

    def bra(side, site, part, acc, dst):
        bra_last(
            tile, pitch, *part, inner, stack_of(am if side else at, site, 2), acc, dst
        )

    m_wide[...] = jnp.zeros_like(m_wide)
    zero = jnp.zeros((tile, tile), jnp.float32)
    for w in range(width, padded):
        for buffer, s in ((mid, 0), (mid, 1), (mid_bra, 0), (mid_ket, 0)):
            buffer[pl.ds((s * padded + w) * pitch, tile), :] = zero
    r_own = pieces("bond", rin_hbm, r_one.at[0], 0, {"sector": down})
    p_own = pieces("bra", p_send.at[0], p_recv.at[0], 1, {"sector": up})
    pl.semaphore_wait(barrier, greeted)
    r_own.start_all(ahead)
    for i in range(3):
        loads[i].wait()
    widen(0)
    prepare_tensor(0, 3)
    prepare_mpo(0, 0, 2)
    loads[3].wait()
    first(0, lin, 0, 2, every, mid)
    for c in range(SLICES):
        second(0, 0, 2, tall(c), mid, acc_one, False)
        emit(pitch, every, tall(c), acc_one, None, p_send.at[0])
        p_own.start(c, ahead)

    def clear(*buffers):
        def body(w, carry):
            for buffer in buffers:
                for step in range(2):
                    buffer[step, w] = jnp.zeros((tile, tile), jnp.bfloat16)
            return carry

        lax.fori_loop(0, width, body, 0)

    @pl.when(jnp.logical_not(below))
    def _():
        clear(p_recv, s_recv)

    @pl.when(jnp.logical_not(above))
    def _():
        clear(r_one)

    @pl.when(sector >= sector_count - 2)
    def _():
        clear(r_two)

    for t in range(3):
        prepare_tensor(0, t)
    widen(1)
    for t in range(4):
        prepare_tensor(1, t)
    for side in range(2):
        for site in range(sites):
            for n in range(3):
                if (side, site, n) != (0, 0, 2):
                    prepare_mpo(side, site, n)

    both(0, lin, 0, 1, acc_one, False)
    loads[4].wait()
    both(1, rin, 1, 0, acc_right, False)

    r_own.start_all(jnp.logical_not(ahead))
    p_own.start_all(jnp.logical_not(ahead))
    s_own = pieces("bra", s_send.at[0], s_recv.at[0], 2, {"sector": up})
    r_pass = pieces("bond", r_one.at[0], r_two.at[0], 3, {"sector": down})

    def on_partial(c):
        p_own.wait_recv(c)
        emit(pitch, every, tall(c), acc_one, p_recv.at[0], s_send.at[0])
        s_own.start(c)

    def on_right(c):
        r_own.wait_recv(c)
        r_pass.start(c)

    in_order((bond_ends, on_right), (bra_ends, on_partial))
    both(0, lin, 0, 0, acc_zero, False)
    both(1, r_one.at[0], 1, 1, acc_right, True)

    def on_sum(c):
        s_own.wait_recv(c)
        emit(pitch, every, tall(c), acc_zero, s_recv.at[0], left_out.at[0])
        ket(0, left_out.at[0], 1, tall(c))

    def on_second_right(c):
        r_pass.wait_recv(c)
        first(1, r_two.at[0], 1, 2, wide(c), mid_bra)

    in_order((bond_ends, on_second_right), (bra_ends, on_sum))
    streams = [r_own, p_own, s_own, r_pass]

    p_own = pieces("bond", p_send.at[1], p_recv.at[1], 5, {"sector": up})
    r_own = pieces("bra", right_out.at[1], r_one.at[1], 4, {"sector": down})

    def send_partial(c):
        bra(0, 1, wide(c), None, p_send.at[1])
        p_own.start(c)

    def send_right(c):
        second(1, 1, 2, tall(c), mid_bra, acc_right, True)
        emit(pitch, every, tall(c), acc_right, None, right_out.at[1])
        r_own.start(c)

    in_order((bond_ends, send_partial), (bra_ends, send_right))

    both(0, left_out.at[0], 1, 1, acc_one, False)
    both(1, right_out.at[1], 0, 0, acc_right, False)
    s_own = pieces("bond", s_send.at[1], s_recv.at[1], 6, {"sector": up})
    r_pass = pieces("bra", r_one.at[1], r_two.at[1], 7, {"sector": down})
    edges = Stream(
        [
            piece("bond", left_out.at[1], edge_out, 8, c, {"chain": after})
            for c in range(chunks)
        ],
        later,
        earlier,
    )

    def on_partial(c):
        p_own.wait_recv(c)
        emit(pitch, wide(c), whole, acc_one, p_recv.at[1], s_send.at[1])
        s_own.start(c)

    def on_right(c):
        r_own.wait_recv(c)
        r_pass.start(c)

    in_order((bra_ends, on_right), (bond_ends, on_partial))
    both(0, left_out.at[0], 1, 0, acc_zero, False)

    def on_sum(c):
        s_own.wait_recv(c)
        emit(pitch, wide(c), whole, acc_zero, s_recv.at[1], left_out.at[1])

        edges.start(c)

    def on_second_right(c):
        r_pass.wait_recv(c)
        ket(1, r_two.at[1], 0, tall(c))

    on_sum(0)
    on_sum(1)
    on_sum(2)
    first(1, r_one.at[1], 0, 1, every, mid)
    on_sum(3)
    quarters = [(i * tile // 4, tile // 4) for i in range(4)]
    for i in range(2):
        second(1, 0, 1, quarters[i], mid, acc_right, True)
    on_sum(4)
    for i in range(2, 4):
        second(1, 0, 1, quarters[i], mid, acc_right, True)
    done = bond_ends[4]
    ends = [(end - done) / (1 - done) for end in bond_ends[5:]]
    in_order((ends, lambda c: on_sum(c + 5)), (bra_ends, on_second_right))
    bra(1, 0, every, acc_right, right_out.at[0])
    streams += [r_own, p_own, s_own, r_pass]

    @pl.when(chain == 0)
    def _():
        keep_edge.wait()

    edges.wait_all()
    edges.finish()
    for stream in streams:
        stream.finish()


def leave(left, right, edge):
    def body(left, right, edge, left_out, right_out, edge_out, sem):
        pairs = [(edge, edge_out.at[0, 0])]
        for src, dst in ((left, left_out), (right, right_out)):
            pairs += [(src.at[i], dst.at[i, 0]) for i in range(src.shape[0])]
        third = edge.shape[0] // PARTS
        cuts = [pl.ds(i * third, third) for i in range(PARTS)]
        pairs = [(src.at[cut], dst.at[cut]) for src, dst in pairs for cut in cuts]
        copies = [
            pltpu.make_async_copy(src, dst, sem.at[i])
            for i, (src, dst) in enumerate(pairs)
        ]
        for copy in copies:
            copy.start()
        for copy in copies:
            copy.wait()

    env = edge.shape
    sites = left.shape[0]
    hbm = pl.BlockSpec(memory_space=pl.ANY)
    return pl.pallas_call(
        body,
        out_shape=(
            jax.ShapeDtypeStruct((sites, 1) + env, left.dtype),
            jax.ShapeDtypeStruct((sites, 1) + env, left.dtype),
            jax.ShapeDtypeStruct((1, 1) + env, left.dtype),
        ),
        in_specs=[pl.BlockSpec(memory_space=pltpu.VMEM)] * 3,
        out_specs=[hbm] * 3,
        scratch_shapes=[pltpu.SemaphoreType.DMA((PARTS * (2 * sites + 1),))],
        compiler_params=pltpu.CompilerParams(vmem_limit_bytes=16 << 20),
    )(left, right, edge)


def shards(chain_count, sector_count, site_tensors, mpo, left_in, right_in, tile_rows):
    sites, _, tile, phys, _ = site_tensors.shape
    width = mpo.shape[1]
    padded = -(-width // 16) * 16
    pitch = tile + PITCH_EXTRA
    tensors = site_tensors.reshape(sites, tile * phys, tile)
    flat_mpo = mpo.transpose(0, 1, 3, 4, 2).reshape(sites, width * 16, width)
    env = (width, tile, tile)
    sizes = (chain_count, sector_count, sites, width, tile, padded, pitch)
    vmem = pl.BlockSpec(memory_space=pltpu.VMEM)
    hbm = pl.BlockSpec(memory_space=pl.ANY)
    streams = 4 * sites + 1
    most = max(SLICES, len(chunks_of(width)))
    left, right, edge = pl.pallas_call(
        functools.partial(kernel, sizes),
        out_shape=(
            pltpu.VMEM((sites,) + env, jnp.bfloat16),
            pltpu.VMEM((sites,) + env, jnp.bfloat16),
            pltpu.VMEM(env, jnp.bfloat16),
        ),
        in_specs=[hbm] * 5,
        out_specs=[vmem] * 3,
        scratch_shapes=[pltpu.VMEM(env, jnp.bfloat16)] * 2
        + [pltpu.VMEM((sites,) + env, jnp.bfloat16)] * 6
        + [
            pltpu.VMEM((2 * padded * pitch, tile), jnp.float32),
        ]
        + [pltpu.VMEM((padded * pitch, tile), jnp.float32)] * 6
        + [
            pltpu.VMEM((sites, phys, tile, tile), jnp.bfloat16),
            pltpu.VMEM((sites, phys, tile, tile), jnp.bfloat16),
            pltpu.VMEM((2, sites, 2, padded, tile), jnp.bfloat16),
            pltpu.VMEM((2, sites, 2 * padded, tile), jnp.bfloat16),
            pltpu.VMEM((sites, phys * tile, tile), jnp.bfloat16),
            pltpu.VMEM((sites, 16 * width, width), jnp.bfloat16),
            pltpu.VMEM((sites, phys * tile, tile), jnp.float32),
            pltpu.VMEM((sites, 16 * padded, tile), jnp.float32),
            pltpu.SMEM(tile_rows.shape, tile_rows.dtype),
            pltpu.SemaphoreType.DMA((streams, most)),
            pltpu.SemaphoreType.DMA((streams, most)),
            pltpu.SemaphoreType.DMA((6,)),
        ],
        compiler_params=pltpu.CompilerParams(
            collective_id=0, has_side_effects=True, vmem_limit_bytes=52 << 20
        ),
    )(tile_rows, tensors, flat_mpo, left_in[0, 0], right_in[0, 0])
    return leave(left, right, edge)


def solution(mesh):
    envs = P("chain", "sector", None, None, None)
    return jax.shard_map(
        functools.partial(shards, mesh.shape["chain"], mesh.shape["sector"]),
        mesh=mesh,
        in_specs=(envs, P("chain", None, None, None, None), envs, envs, P()),
        out_specs=(envs, envs, envs),
        check_vma=False,
    )
```

```python
import functools

import jax
import jax.numpy as jnp
from jax import lax
from jax.experimental import pallas as pl
from jax.experimental.pallas import tpu as pltpu
from jax.sharding import PartitionSpec as P

groups = ((0, 1), (1, 3), (3, 4))
charge = (0, 1, 1, 2)
SLICES = 8
SPAN = 6
ENDS = (2, 4)
PITCH_EXTRA = 8
LEAD = 0.9
PARTS = 1
ROWS = 16
PAIRS = 3


def stage_one(tile, padded, pitch, start, width, src, lhs, mid):
    count = lhs.shape[0] // tile
    pairs = width // 2
    unroll = max(n for n in range(1, PAIRS + 1) if pairs % n == 0)

    def body(i, carry):
        for k in range(unroll):
            w = start + (i * unroll + k) * 2
            rhs = jnp.concatenate([src[w], src[w + 1]], axis=1)
            prod = jnp.dot(lhs, rhs, preferred_element_type=jnp.float32)
            for s in range(count):
                for j in range(2):
                    row = pl.multiple_of((s * padded + w + j) * pitch, 8)
                    mid[pl.ds(row, tile), :] = prod[
                        s * tile : (s + 1) * tile, j * tile : (j + 1) * tile
                    ]
        return carry

    lax.fori_loop(0, pairs // unroll, body, 0)


def stage_two(tile, padded, pitch, start, rows, mid, mpo_part, fin, out, add):
    count = fin.shape[0] // tile

    def block(i, carry):
        base = start + i * ROWS
        left = []
        for j in range(0, ROWS, 2):
            both = [
                mid[pl.ds(base + j + k, count * padded, stride=pitch), :].astype(
                    jnp.bfloat16
                )
                for k in range(2)
            ]
            inner = jnp.dot(
                mpo_part,
                jnp.concatenate(both, axis=1),
                preferred_element_type=jnp.float32,
            ).astype(jnp.bfloat16)
            for k in range(2):
                left.append(
                    jnp.concatenate(
                        [
                            inner[
                                t * padded : (t + 1) * padded,
                                k * tile : (k + 1) * tile,
                            ]
                            for t in range(count)
                        ],
                        axis=1,
                    )
                )
        prod = jnp.dot(
            jnp.concatenate(left, axis=0), fin, preferred_element_type=jnp.float32
        )
        for j in range(ROWS):
            spot = pl.ds(base + j, padded, stride=pitch)
            value = prod[j * padded : (j + 1) * padded]
            if add:
                value = value + out[spot, :]
            out[spot, :] = value
        return carry

    lax.fori_loop(0, rows // ROWS, block, 0)


def ket_first(width, padded, pitch, start, rows, src, fin, mpo_part, mid, inner):
    group = max(n for n in range(1, 43) if width % n == 0)

    def body(i, carry):
        first = i * group
        block = src[pl.ds(first, group), start : start + rows, :]
        prod = jnp.dot(
            block.reshape(group * rows, block.shape[2]),
            fin,
            preferred_element_type=jnp.float32,
        )
        for k in range(group):
            row = pl.multiple_of((first + k) * pitch + start, 8)
            mid[pl.ds(row, rows), :] = prod[k * rows : (k + 1) * rows]
        return carry

    lax.fori_loop(0, width // group, body, 0)
    tile = fin.shape[1]

    def block(i, carry):
        for j in range(0, ROWS, 2):
            base = start + i * ROWS + j
            both = [
                mid[pl.ds(base + k, padded, stride=pitch), :].astype(jnp.bfloat16)
                for k in range(2)
            ]
            prod = jnp.dot(
                mpo_part,
                jnp.concatenate(both, axis=1),
                preferred_element_type=jnp.float32,
            )
            for k in range(2):
                inner[pl.ds(base + k, padded, stride=pitch), :] = prod[
                    :, k * tile : (k + 1) * tile
                ]
        return carry

    lax.fori_loop(0, rows // ROWS, block, 0)


def bra_last(tile, pitch, start, width, inner, lhs, acc, dst):
    for w in range(start, start + width, 2):
        rows = [pl.ds((w + k) * pitch, tile) for k in range(2)]
        rhs = jnp.concatenate(
            [inner[row, :].astype(jnp.bfloat16) for row in rows], axis=1
        )
        prod = jnp.dot(lhs, rhs, preferred_element_type=jnp.float32)
        for k in range(2):
            value = prod[:, k * tile : (k + 1) * tile]
            if acc is not None:
                value = value + acc[rows[k], :]
            dst[w + k] = value.astype(jnp.bfloat16)


def emit(pitch, wide, tall, acc, other, dst):
    first, width = wide
    start, rows = tall

    def one(i, carry):
        for k in range(2):
            w = first + 2 * i + k
            value = acc[pl.ds(pl.multiple_of(w * pitch + start, 8), rows), :]
            if other is not None:
                value = value + other[w, start : start + rows, :].astype(jnp.float32)
            dst[w, start : start + rows, :] = value.astype(jnp.bfloat16)
        return carry

    lax.fori_loop(0, width // 2, one, 0)


def chunks_of(width):
    middle = width - 2 * sum(ENDS)
    spans = list(ENDS) + [SPAN] * (middle // SPAN) + [middle % SPAN] + list(ENDS[::-1])
    spans = [span for span in spans if span]
    return [(sum(spans[:i]), span) for i, span in enumerate(spans)]


def in_order(*lists):
    spots = []
    for at, (ends, act) in enumerate(lists):
        spots += [(end, at, c, act) for c, end in enumerate(ends)]
    for _, _, c, act in sorted(spots, key=lambda spot: spot[:3]):
        act(c)


class Stream:
    def __init__(self, copies, total, send, receive):
        self.copies, self.total = copies, total
        self.send, self.receive = send, receive

    def start(self, c, also=None):
        send = self.send if also is None else jnp.logical_and(self.send, also)
        pl.when(send)(self.copies[c].start)

    def start_all(self, also):
        @pl.when(jnp.logical_and(self.send, also))
        def _():
            for copy in self.copies:
                copy.start()

    def wait_recv(self, c):
        pl.when(self.receive)(self.copies[c].wait_recv)

    def wait_all(self):
        @pl.when(self.receive)
        def _():
            for copy in self.copies:
                copy.wait_recv()

    def finish(self):
        pl.when(self.send)(self.total.wait_send)


def kernel(
    sizes,
    rows_hbm, a_hbm, m_hbm, lin_hbm, rin_hbm,
    left_out, right_out, edge_out,
    lin, rin, r_one, r_two, p_send, p_recv, s_send, s_recv,
    mid, mid_bra, mid_ket, inner, acc_one, acc_zero, acc_right,
    am, at, m_one, m_two, a_in, m_in, a_wide, m_wide, rows_ref,
    send_sem, recv_sem, load_sem,
):
    chain_count, sector_count, sites, width, tile, padded, pitch = sizes
    chain = lax.axis_index("chain")
    sector = lax.axis_index("sector")
    up = lax.rem(sector + 1, sector_count)
    down = lax.rem(sector + sector_count - 1, sector_count)
    after = lax.rem(chain + 1, chain_count)
    before = lax.rem(chain + chain_count - 1, chain_count)
    rows = tile // SLICES
    parts = chunks_of(width)
    chunks = len(parts)
    ahead = lax.rem(chain, 2) == 1
    bra_ends = [(c + 1) / SLICES for c in range(SLICES)]
    bond_ends = [sum(part) / width for part in parts]
    above, below = sector < sector_count - 1, sector > 0
    later, earlier = chain < chain_count - 1, chain > 0

    barrier = pltpu.get_barrier_semaphore()
    greeted = jnp.int32(0)
    for known, there in (
        (above, {"sector": up}),
        (below, {"sector": down}),
        (later, {"chain": after}),
        (earlier, {"chain": before}),
    ):

        @pl.when(known)
        def _(there=there):
            pl.semaphore_signal(barrier, inc=1, device_id=there)

        greeted = greeted + jnp.where(known, 1, 0)
    loads = [
        pltpu.make_async_copy(src, dst, load_sem.at[i])
        for i, (src, dst) in enumerate(
            ((rows_hbm, rows_ref), (a_hbm, a_in), (m_hbm, m_in), (lin_hbm, lin), (rin_hbm, rin))
        )
    ]
    for load in loads:
        load.start()
    keep_edge = pltpu.make_async_copy(lin_hbm, edge_out, load_sem.at[5])

    @pl.when(chain == 0)
    def _():
        keep_edge.start()

    forms = ("bond", "bra", "bra", "bond", "bra", "bond", "bond", "bra", "bond")
    counts = {"bond": chunks, "bra": SLICES}
    starts = [sum(counts[form] for form in forms[:i]) for i in range(len(forms))]

    def total(src, dst, stream, there):
        return pltpu.make_async_remote_copy(
            src_ref=src,
            dst_ref=dst,
            send_sem=send_sem.at[stream],
            recv_sem=recv_sem.at[starts[stream]],
            device_id=there,
            device_id_type=pl.DeviceIdType.MESH,
        )

    def piece(src, dst, stream, c, there):
        form = forms[stream]
        if form == "bra":
            cut = (slice(None), pl.ds(c * rows, rows), slice(None))
        else:
            cut = (pl.ds(*parts[c]), slice(None), slice(None))
        return pltpu.make_async_remote_copy(
            src_ref=src.at[cut],
            dst_ref=dst.at[cut],
            send_sem=send_sem.at[stream],
            recv_sem=recv_sem.at[starts[stream] + c],
            device_id=there,
            device_id_type=pl.DeviceIdType.MESH,
        )

    def pieces(src, dst, stream, there):
        count = counts[forms[stream]]
        copies = [piece(src, dst, stream, c, there) for c in range(count)]
        send, receive = (
            (below, above),
            (above, below),
            (above, below),
            (below & above, sector < sector_count - 2),
            (later, earlier),
        )[stream % 4 if stream < 8 else 4]
        return Stream(copies, total(src, dst, stream, there), send, receive)

    ids_a = lax.broadcasted_iota(jnp.int32, (tile, tile), 0)
    ids_b = lax.broadcasted_iota(jnp.int32, (tile, tile), 1)

    def widen(site):
        a_wide[site] = a_in[site].astype(jnp.float32)
        m_wide[site, 0 : 16 * width, 0:width] = m_in[site].astype(jnp.float32)

    def prepare_tensor(site, t):
        bond = chain * sites + site
        there = sector + charge[t]
        seen = rows_ref[bond + 1, jnp.minimum(there, sector_count - 1)]
        high = jnp.where(there < sector_count, seen, 0)
        keep = (ids_a < rows_ref[bond, sector]) & (ids_b < high)
        value = jnp.where(keep, a_wide[site, pl.ds(t, tile, stride=4), :], 0.0)
        am[site, t] = value.astype(jnp.bfloat16)
        at[site, t] = value.T.astype(jnp.bfloat16)

    def corner(side, site, s, t):
        value = m_wide[site, pl.ds(4 * s + t, padded, stride=16), :]
        if side == 0:
            full = jnp.concatenate(
                [value, jnp.zeros((tile - padded, tile), jnp.float32)], axis=0
            )
            value = full.T[:padded]
        return value

    def prepare_mpo(side, site, n):
        lo, hi = groups[n]
        for t in range(lo, hi):
            value = corner(side, site, lo, t)
            for s in range(lo + 1, hi):
                value = value + pltpu.roll(
                    corner(side, site, s, t), (s - lo) * padded, 1
                )
            value = value.astype(jnp.bfloat16)
            if n == 1:
                m_two[side, site, (t - lo) * padded : (t - lo + 1) * padded] = value
            else:
                m_one[side, site, n // 2] = value

    def mpo_of(side, site, n):
        if n == 1:
            return m_two[side, site, :, : 2 * padded]
        return m_one[side, site, n // 2, :, :padded]

    def stack_of(mats, site, n):
        lo, hi = groups[n]
        return mats[site, lo:hi].reshape((hi - lo) * tile, tile)

    one = functools.partial(stage_one, tile, padded, pitch)
    two = functools.partial(stage_two, tile, padded, pitch)
    every = (0, width)
    whole = (0, tile)

    def tall(c):
        return (c * rows, rows)

    def wide(c):
        return parts[c]

    def first(side, src, site, n, part, dst):
        one(*part, src, stack_of(am if side else at, site, n), dst)

    def second(side, site, n, part, src, acc, add):
        two(
            *part, src, mpo_of(side, site, n),
            stack_of(at if side else am, site, n), acc, add,
        )

    def both(side, src, site, n, acc, add):
        first(side, src, site, n, every, mid)
        second(side, site, n, whole, mid, acc, add)

    def ket(side, src, site, part):
        ket_first(
            width, padded, pitch, *part, src, stack_of(at if side else am, site, 2),
            mpo_of(side, site, 2), mid_ket, inner,
        )

    def bra(side, site, part, acc, dst):
        bra_last(
            tile, pitch, *part, inner, stack_of(am if side else at, site, 2), acc, dst
        )

    m_wide[...] = jnp.zeros_like(m_wide)
    zero = jnp.zeros((tile, tile), jnp.float32)
    for w in range(width, padded):
        for buffer, s in ((mid, 0), (mid, 1), (mid_bra, 0), (mid_ket, 0)):
            buffer[pl.ds((s * padded + w) * pitch, tile), :] = zero
    r_own = pieces(rin_hbm, r_one.at[0], 0, {"sector": down})
    p_own = pieces(p_send.at[0], p_recv.at[0], 1, {"sector": up})
    for i in range(3):
        loads[i].wait()
    widen(0)
    prepare_tensor(0, 3)
    prepare_mpo(0, 0, 2)
    loads[3].wait()
    most = width // (4 * PAIRS) * 2 * PAIRS
    first(0, lin, 0, 2, (0, most), mid)
    pl.semaphore_wait(barrier, greeted)
    r_own.start_all(ahead)
    first(0, lin, 0, 2, (most, width - most), mid)
    for c in range(SLICES):
        second(0, 0, 2, tall(c), mid, acc_one, False)
        emit(pitch, every, tall(c), acc_one, None, p_send.at[0])
        p_own.start(c, ahead)

    def clear(*buffers):
        def body(w, carry):
            for buffer in buffers:
                for step in range(2):
                    buffer[step, w] = jnp.zeros((tile, tile), jnp.bfloat16)
            return carry

        lax.fori_loop(0, width, body, 0)

    @pl.when(jnp.logical_not(below))
    def _():
        clear(p_recv, s_recv)

    @pl.when(jnp.logical_not(above))
    def _():
        clear(r_one)

    @pl.when(sector >= sector_count - 2)
    def _():
        clear(r_two)

    for t in range(3):
        prepare_tensor(0, t)
    widen(1)
    for t in range(4):
        prepare_tensor(1, t)
    for side in range(2):
        for site in range(sites):
            for n in range(3):
                if (side, site, n) != (0, 0, 2):
                    prepare_mpo(side, site, n)

    both(0, lin, 0, 1, acc_one, False)
    loads[4].wait()
    both(1, rin, 1, 0, acc_right, False)

    r_own.start_all(jnp.logical_not(ahead))
    p_own.start_all(jnp.logical_not(ahead))
    s_own = pieces(s_send.at[0], s_recv.at[0], 2, {"sector": up})
    r_pass = pieces(r_one.at[0], r_two.at[0], 3, {"sector": down})

    def on_partial(c):
        p_own.wait_recv(c)
        emit(pitch, every, tall(c), acc_one, p_recv.at[0], s_send.at[0])
        s_own.start(c)

    def on_right(c):
        r_own.wait_recv(c)
        r_pass.start(c)

    in_order((bond_ends, on_right), (bra_ends, on_partial))
    both(0, lin, 0, 0, acc_zero, False)
    both(1, r_one.at[0], 1, 1, acc_right, True)

    def on_sum(c):
        s_own.wait_recv(c)
        emit(pitch, every, tall(c), acc_zero, s_recv.at[0], left_out.at[0])
        ket(0, left_out.at[0], 1, tall(c))

    def on_second_right(c):
        r_pass.wait_recv(c)
        first(1, r_two.at[0], 1, 2, wide(c), mid_bra)

    in_order((bond_ends, on_second_right), (bra_ends, on_sum))
    for stream in (r_own, p_own):
        stream.finish()
    early = (s_own, r_pass)

    p_own = pieces(p_send.at[1], p_recv.at[1], 5, {"sector": up})
    r_own = pieces(right_out.at[1], r_one.at[1], 4, {"sector": down})

    def send_partial(c):
        bra(0, 1, wide(c), None, p_send.at[1])
        p_own.start(c)

    def send_right(c):
        second(1, 1, 2, tall(c), mid_bra, acc_right, True)
        emit(pitch, every, tall(c), acc_right, None, right_out.at[1])
        r_own.start(c)

    in_order((bond_ends, send_partial), (bra_ends, send_right))

    both(0, left_out.at[0], 1, 1, acc_one, False)
    both(1, right_out.at[1], 0, 0, acc_right, False)
    s_own = pieces(s_send.at[1], s_recv.at[1], 6, {"sector": up})
    r_pass = pieces(r_one.at[1], r_two.at[1], 7, {"sector": down})
    edges = pieces(left_out.at[1], edge_out, 8, {"chain": after})

    def on_partial(c):
        p_own.wait_recv(c)
        emit(pitch, wide(c), whole, acc_one, p_recv.at[1], s_send.at[1])
        s_own.start(c)

    def on_right(c):
        r_own.wait_recv(c)
        r_pass.start(c)

    in_order((bra_ends, on_right), (bond_ends, on_partial))
    both(0, left_out.at[0], 1, 0, acc_zero, False)

    def on_sum(c):
        s_own.wait_recv(c)
        emit(pitch, wide(c), whole, acc_zero, s_recv.at[1], left_out.at[1])

        edges.start(c)

    def on_second_right(c):
        r_pass.wait_recv(c)
        ket(1, r_two.at[1], 0, tall(c))

    for stream in early + (r_own, p_own):
        stream.finish()
    on_sum(0)
    on_sum(1)
    on_sum(2)
    first(1, r_one.at[1], 0, 1, every, mid)
    on_sum(3)
    quarters = [(i * tile // 4, tile // 4) for i in range(4)]
    for i in range(2):
        second(1, 0, 1, quarters[i], mid, acc_right, True)
    on_sum(4)
    for i in range(2, 4):
        second(1, 0, 1, quarters[i], mid, acc_right, True)
    done = bond_ends[4]
    ends = [(end - done) / (1 - done) for end in bond_ends[5:]]

    def on_last_right(c):
        if c < SLICES:
            on_second_right(c)
        else:
            bra(1, 0, every, acc_right, right_out.at[0])

    lead = [LEAD * end for end in bra_ends] + [LEAD]
    in_order((lead, on_last_right), (ends, lambda c: on_sum(c + 5)))

    @pl.when(chain == 0)
    def _():
        keep_edge.wait()

    edges.wait_all()
    edges.finish()
    for stream in (s_own, r_pass):
        stream.finish()


def leave(left, right, edge):
    def body(left, right, edge, left_out, right_out, edge_out, sem):
        pairs = [(edge, edge_out.at[0, 0])]
        for src, dst in ((left, left_out), (right, right_out)):
            pairs += [(src.at[i], dst.at[i, 0]) for i in range(src.shape[0])]
        third = edge.shape[0] // PARTS
        cuts = [pl.ds(i * third, third) for i in range(PARTS)]
        pairs = [(src.at[cut], dst.at[cut]) for src, dst in pairs for cut in cuts]
        copies = [
            pltpu.make_async_copy(src, dst, sem.at[i])
            for i, (src, dst) in enumerate(pairs)
        ]
        for copy in copies:
            copy.start()
        for copy in copies:
            copy.wait()

    env = edge.shape
    sites = left.shape[0]
    hbm = pl.BlockSpec(memory_space=pl.ANY)
    return pl.pallas_call(
        body,
        out_shape=(
            jax.ShapeDtypeStruct((sites, 1) + env, left.dtype),
            jax.ShapeDtypeStruct((sites, 1) + env, left.dtype),
            jax.ShapeDtypeStruct((1, 1) + env, left.dtype),
        ),
        in_specs=[pl.BlockSpec(memory_space=pltpu.VMEM)] * 3,
        out_specs=[hbm] * 3,
        scratch_shapes=[pltpu.SemaphoreType.DMA((PARTS * (2 * sites + 1),))],
        compiler_params=pltpu.CompilerParams(vmem_limit_bytes=16 << 20),
    )(left, right, edge)


def shards(chain_count, sector_count, site_tensors, mpo, left_in, right_in, tile_rows):
    sites, _, tile, phys, _ = site_tensors.shape
    width = mpo.shape[1]
    padded = -(-width // 16) * 16
    pitch = tile + PITCH_EXTRA
    tensors = site_tensors.reshape(sites, tile * phys, tile)
    flat_mpo = mpo.transpose(0, 1, 3, 4, 2).reshape(sites, width * 16, width)
    env = (width, tile, tile)
    sizes = (chain_count, sector_count, sites, width, tile, padded, pitch)
    vmem = pl.BlockSpec(memory_space=pltpu.VMEM)
    hbm = pl.BlockSpec(memory_space=pl.ANY)
    left, right, edge = pl.pallas_call(
        functools.partial(kernel, sizes),
        out_shape=(
            pltpu.VMEM((sites,) + env, jnp.bfloat16),
            pltpu.VMEM((sites,) + env, jnp.bfloat16),
            pltpu.VMEM(env, jnp.bfloat16),
        ),
        in_specs=[hbm] * 5,
        out_specs=[vmem] * 3,
        scratch_shapes=[pltpu.VMEM(env, jnp.bfloat16)] * 2
        + [pltpu.VMEM((sites,) + env, jnp.bfloat16)] * 6
        + [
            pltpu.VMEM((2 * padded * pitch, tile), jnp.float32),
        ]
        + [pltpu.VMEM((padded * pitch, tile), jnp.float32)] * 6
        + [
            pltpu.VMEM((sites, phys, tile, tile), jnp.bfloat16),
            pltpu.VMEM((sites, phys, tile, tile), jnp.bfloat16),
            pltpu.VMEM((2, sites, 2, padded, tile), jnp.bfloat16),
            pltpu.VMEM((2, sites, 2 * padded, tile), jnp.bfloat16),
            pltpu.VMEM((sites, phys * tile, tile), jnp.bfloat16),
            pltpu.VMEM((sites, 16 * width, width), jnp.bfloat16),
            pltpu.VMEM((sites, phys * tile, tile), jnp.float32),
            pltpu.VMEM((sites, 16 * padded, tile), jnp.float32),
            pltpu.SMEM(tile_rows.shape, tile_rows.dtype),
            pltpu.SemaphoreType.DMA((9,)),
            pltpu.SemaphoreType.DMA((4 * SLICES + 5 * len(chunks_of(width)),)),
            pltpu.SemaphoreType.DMA((6,)),
        ],
        compiler_params=pltpu.CompilerParams(
            collective_id=0, has_side_effects=True, vmem_limit_bytes=52 << 20
        ),
    )(tile_rows, tensors, flat_mpo, left_in[0, 0], right_in[0, 0])
    return leave(left, right, edge)


def solution(mesh):
    envs = P("chain", "sector", None, None, None)
    return jax.shard_map(
        functools.partial(shards, mesh.shape["chain"], mesh.shape["sector"]),
        mesh=mesh,
        in_specs=(envs, P("chain", None, None, None, None), envs, envs, P()),
        out_specs=(envs, envs, envs),
        check_vma=False,
    )
```

```python
import functools

import jax
import jax.numpy as jnp
from jax import lax
from jax.experimental import pallas as pl
from jax.experimental.pallas import tpu as pltpu
from jax.sharding import PartitionSpec as P

groups = ((0, 1), (1, 3), (3, 4))
charge = (0, 1, 1, 2)
SLICES = 8
SPAN = 6
ENDS = (2, 4)
PITCH_EXTRA = 8
LEAD = 0.9
PARTS = 1
ROWS = 16
PAIRS = 3


def stage_one(tile, padded, pitch, start, width, src, lhs, mid):
    count = lhs.shape[0] // tile
    pairs = width // 2
    unroll = max(n for n in range(1, PAIRS + 1) if pairs % n == 0)

    def body(i, carry):
        for k in range(unroll):
            w = start + (i * unroll + k) * 2
            rhs = jnp.concatenate([src[w], src[w + 1]], axis=1)
            prod = jnp.dot(lhs, rhs, preferred_element_type=jnp.float32)
            for s in range(count):
                for j in range(2):
                    row = pl.multiple_of((s * padded + w + j) * pitch, 8)
                    mid[pl.ds(row, tile), :] = prod[
                        s * tile : (s + 1) * tile, j * tile : (j + 1) * tile
                    ]
        return carry

    lax.fori_loop(0, pairs // unroll, body, 0)


def stage_two(tile, padded, pitch, start, rows, mid, mpo_part, fin, out, add):
    count = fin.shape[0] // tile

    def block(i, carry):
        base = start + i * ROWS
        left = []
        for j in range(0, ROWS, 2):
            both = [
                mid[pl.ds(base + j + k, count * padded, stride=pitch), :].astype(
                    jnp.bfloat16
                )
                for k in range(2)
            ]
            inner = jnp.dot(
                mpo_part,
                jnp.concatenate(both, axis=1),
                preferred_element_type=jnp.float32,
            ).astype(jnp.bfloat16)
            for k in range(2):
                left.append(
                    jnp.concatenate(
                        [
                            inner[
                                t * padded : (t + 1) * padded,
                                k * tile : (k + 1) * tile,
                            ]
                            for t in range(count)
                        ],
                        axis=1,
                    )
                )
        prod = jnp.dot(
            jnp.concatenate(left, axis=0), fin, preferred_element_type=jnp.float32
        )
        for j in range(ROWS):
            spot = pl.ds(base + j, padded, stride=pitch)
            value = prod[j * padded : (j + 1) * padded]
            if add:
                value = value + out[spot, :]
            out[spot, :] = value
        return carry

    lax.fori_loop(0, rows // ROWS, block, 0)


def ket_first(width, padded, pitch, start, rows, src, fin, mpo_part, mid, inner):
    group = max(n for n in range(1, 43) if width % n == 0)

    def body(i, carry):
        first = i * group
        block = src[pl.ds(first, group), start : start + rows, :]
        prod = jnp.dot(
            block.reshape(group * rows, block.shape[2]),
            fin,
            preferred_element_type=jnp.float32,
        )
        for k in range(group):
            row = pl.multiple_of((first + k) * pitch + start, 8)
            mid[pl.ds(row, rows), :] = prod[k * rows : (k + 1) * rows]
        return carry

    lax.fori_loop(0, width // group, body, 0)
    tile = fin.shape[1]

    def block(i, carry):
        for j in range(0, ROWS, 2):
            base = start + i * ROWS + j
            both = [
                mid[pl.ds(base + k, padded, stride=pitch), :].astype(jnp.bfloat16)
                for k in range(2)
            ]
            prod = jnp.dot(
                mpo_part,
                jnp.concatenate(both, axis=1),
                preferred_element_type=jnp.float32,
            )
            for k in range(2):
                inner[pl.ds(base + k, padded, stride=pitch), :] = prod[
                    :, k * tile : (k + 1) * tile
                ]
        return carry

    lax.fori_loop(0, rows // ROWS, block, 0)


def bra_last(tile, pitch, start, width, inner, lhs, acc, dst):
    for w in range(start, start + width, 2):
        rows = [pl.ds((w + k) * pitch, tile) for k in range(2)]
        rhs = jnp.concatenate(
            [inner[row, :].astype(jnp.bfloat16) for row in rows], axis=1
        )
        prod = jnp.dot(lhs, rhs, preferred_element_type=jnp.float32)
        for k in range(2):
            value = prod[:, k * tile : (k + 1) * tile]
            if acc is not None:
                value = value + acc[rows[k], :]
            dst[w + k] = value.astype(jnp.bfloat16)


def emit(pitch, wide, tall, acc, other, dst):
    first, width = wide
    start, rows = tall

    def one(i, carry):
        for k in range(2):
            w = first + 2 * i + k
            value = acc[pl.ds(pl.multiple_of(w * pitch + start, 8), rows), :]
            if other is not None:
                value = value + other[w, start : start + rows, :].astype(jnp.float32)
            dst[w, start : start + rows, :] = value.astype(jnp.bfloat16)
        return carry

    lax.fori_loop(0, width // 2, one, 0)


def chunks_of(width):
    middle = width - 2 * sum(ENDS)
    spans = list(ENDS) + [SPAN] * (middle // SPAN) + [middle % SPAN] + list(ENDS[::-1])
    spans = [span for span in spans if span]
    return [(sum(spans[:i]), span) for i, span in enumerate(spans)]


def in_order(*lists):
    spots = []
    for at, (ends, act) in enumerate(lists):
        spots += [(end, at, c, act) for c, end in enumerate(ends)]
    for _, _, c, act in sorted(spots, key=lambda spot: spot[:3]):
        act(c)


class Stream:
    def __init__(self, copies, total, send, receive):
        self.copies, self.total = copies, total
        self.send, self.receive = send, receive

    def start(self, c, also=None):
        send = self.send if also is None else jnp.logical_and(self.send, also)
        pl.when(send)(self.copies[c].start)

    def start_all(self, also):
        @pl.when(jnp.logical_and(self.send, also))
        def _():
            for copy in self.copies:
                copy.start()

    def wait_recv(self, c):
        pl.when(self.receive)(self.copies[c].wait_recv)

    def wait_all(self):
        @pl.when(self.receive)
        def _():
            for copy in self.copies:
                copy.wait_recv()

    def finish(self):
        pl.when(self.send)(self.total.wait_send)


def kernel(
    sizes,
    rows_hbm, a_hbm, m_hbm, lin_hbm, rin_hbm,
    left_out, right_out, edge_out,
    lin, rin, r_one, r_two, p_send, p_recv, s_send, s_recv,
    mid, mid_bra, mid_ket, inner, acc_one, acc_zero, acc_right,
    am, at, m_one, m_two, a_in, m_in, a_wide, m_wide, rows_ref,
    send_sem, recv_sem, load_sem,
):
    chain_count, sector_count, sites, width, tile, padded, pitch = sizes
    chain = lax.axis_index("chain")
    sector = lax.axis_index("sector")
    up = lax.rem(sector + 1, sector_count)
    down = lax.rem(sector + sector_count - 1, sector_count)
    after = lax.rem(chain + 1, chain_count)
    before = lax.rem(chain + chain_count - 1, chain_count)
    rows = tile // SLICES
    parts = chunks_of(width)
    chunks = len(parts)
    ahead = lax.rem(chain, 2) == 1
    bra_ends = [(c + 1) / SLICES for c in range(SLICES)]
    bond_ends = [sum(part) / width for part in parts]
    above, below = sector < sector_count - 1, sector > 0
    later, earlier = chain < chain_count - 1, chain > 0

    barrier = pltpu.get_barrier_semaphore()
    greeted = jnp.int32(0)
    for known, there in (
        (above, {"sector": up}),
        (below, {"sector": down}),
        (later, {"chain": after}),
        (earlier, {"chain": before}),
    ):

        @pl.when(known)
        def _(there=there):
            pl.semaphore_signal(barrier, inc=1, device_id=there)

        greeted = greeted + jnp.where(known, 1, 0)
    loads = [
        pltpu.make_async_copy(src, dst, load_sem.at[i])
        for i, (src, dst) in enumerate(
            ((rows_hbm, rows_ref), (a_hbm, a_in), (lin_hbm, lin), (m_hbm, m_in), (rin_hbm, rin))
        )
    ]
    for load in loads[:4]:
        load.start()
    keep_edge = pltpu.make_async_copy(lin_hbm, edge_out, load_sem.at[5])

    forms = ("bond", "bra", "bra", "bond", "bra", "bond", "bond", "bra", "bond")
    counts = {"bond": chunks, "bra": SLICES}
    starts = [sum(counts[form] for form in forms[:i]) for i in range(len(forms))]

    def total(src, dst, stream, there):
        return pltpu.make_async_remote_copy(
            src_ref=src,
            dst_ref=dst,
            send_sem=send_sem.at[stream],
            recv_sem=recv_sem.at[starts[stream]],
            device_id=there,
            device_id_type=pl.DeviceIdType.MESH,
        )

    def piece(src, dst, stream, c, there):
        form = forms[stream]
        if form == "bra":
            cut = (slice(None), pl.ds(c * rows, rows), slice(None))
        else:
            cut = (pl.ds(*parts[c]), slice(None), slice(None))
        return pltpu.make_async_remote_copy(
            src_ref=src.at[cut],
            dst_ref=dst.at[cut],
            send_sem=send_sem.at[stream],
            recv_sem=recv_sem.at[starts[stream] + c],
            device_id=there,
            device_id_type=pl.DeviceIdType.MESH,
        )

    def pieces(src, dst, stream, there):
        count = counts[forms[stream]]
        copies = [piece(src, dst, stream, c, there) for c in range(count)]
        send, receive = (
            (below, above),
            (above, below),
            (above, below),
            (below & above, sector < sector_count - 2),
            (later, earlier),
        )[stream % 4 if stream < 8 else 4]
        return Stream(copies, total(src, dst, stream, there), send, receive)

    ids_a = lax.broadcasted_iota(jnp.int32, (tile, tile), 0)
    ids_b = lax.broadcasted_iota(jnp.int32, (tile, tile), 1)

    def widen_tensor(site):
        a_wide[site] = a_in[site].astype(jnp.float32)

    def widen_mpo(site):
        m_wide[site, 0 : 16 * width, 0:width] = m_in[site].astype(jnp.float32)

    def prepare_tensor(site, t):
        bond = chain * sites + site
        there = sector + charge[t]
        seen = rows_ref[bond + 1, jnp.minimum(there, sector_count - 1)]
        high = jnp.where(there < sector_count, seen, 0)
        keep = (ids_a < rows_ref[bond, sector]) & (ids_b < high)
        value = jnp.where(keep, a_wide[site, pl.ds(t, tile, stride=4), :], 0.0)
        am[site, t] = value.astype(jnp.bfloat16)
        at[site, t] = value.T.astype(jnp.bfloat16)

    def corner(side, site, s, t):
        value = m_wide[site, pl.ds(4 * s + t, padded, stride=16), :]
        if side == 0:
            full = jnp.concatenate(
                [value, jnp.zeros((tile - padded, tile), jnp.float32)], axis=0
            )
            value = full.T[:padded]
        return value

    def prepare_mpo(side, site, n):
        lo, hi = groups[n]
        for t in range(lo, hi):
            value = corner(side, site, lo, t)
            for s in range(lo + 1, hi):
                value = value + pltpu.roll(
                    corner(side, site, s, t), (s - lo) * padded, 1
                )
            value = value.astype(jnp.bfloat16)
            if n == 1:
                m_two[side, site, (t - lo) * padded : (t - lo + 1) * padded] = value
            else:
                m_one[side, site, n // 2] = value

    def mpo_of(side, site, n):
        if n == 1:
            return m_two[side, site, :, : 2 * padded]
        return m_one[side, site, n // 2, :, :padded]

    def stack_of(mats, site, n):
        lo, hi = groups[n]
        return mats[site, lo:hi].reshape((hi - lo) * tile, tile)

    one = functools.partial(stage_one, tile, padded, pitch)
    two = functools.partial(stage_two, tile, padded, pitch)
    every = (0, width)
    whole = (0, tile)

    def tall(c):
        return (c * rows, rows)

    def wide(c):
        return parts[c]

    def first(side, src, site, n, part, dst):
        one(*part, src, stack_of(am if side else at, site, n), dst)

    def second(side, site, n, part, src, acc, add):
        two(
            *part, src, mpo_of(side, site, n),
            stack_of(at if side else am, site, n), acc, add,
        )

    def both(side, src, site, n, acc, add):
        first(side, src, site, n, every, mid)
        second(side, site, n, whole, mid, acc, add)

    def ket(side, src, site, part):
        ket_first(
            width, padded, pitch, *part, src, stack_of(at if side else am, site, 2),
            mpo_of(side, site, 2), mid_ket, inner,
        )

    def bra(side, site, part, acc, dst):
        bra_last(
            tile, pitch, *part, inner, stack_of(am if side else at, site, 2), acc, dst
        )

    m_wide[...] = jnp.zeros_like(m_wide)
    zero = jnp.zeros((tile, tile), jnp.float32)
    for w in range(width, padded):
        for buffer, s in ((mid, 0), (mid, 1), (mid_bra, 0), (mid_ket, 0)):
            buffer[pl.ds((s * padded + w) * pitch, tile), :] = zero
    r_own = pieces(rin_hbm, r_one.at[0], 0, {"sector": down})
    p_own = pieces(p_send.at[0], p_recv.at[0], 1, {"sector": up})
    for i in range(2):
        loads[i].wait()
    widen_tensor(0)
    prepare_tensor(0, 3)
    loads[2].wait()
    most = width // (4 * PAIRS) * 2 * PAIRS
    first(0, lin, 0, 2, (0, most), mid)
    pl.semaphore_wait(barrier, greeted)
    r_own.start_all(ahead)
    first(0, lin, 0, 2, (most, width - most), mid)
    loads[3].wait()
    loads[4].start()

    @pl.when(chain == 0)
    def _():
        keep_edge.start()

    widen_mpo(0)
    prepare_mpo(0, 0, 2)
    for c in range(SLICES):
        second(0, 0, 2, tall(c), mid, acc_one, False)
        emit(pitch, every, tall(c), acc_one, None, p_send.at[0])
        p_own.start(c, ahead)

    def clear(*buffers):
        def body(w, carry):
            for buffer in buffers:
                for step in range(2):
                    buffer[step, w] = jnp.zeros((tile, tile), jnp.bfloat16)
            return carry

        lax.fori_loop(0, width, body, 0)

    @pl.when(jnp.logical_not(below))
    def _():
        clear(p_recv, s_recv)

    @pl.when(jnp.logical_not(above))
    def _():
        clear(r_one)

    @pl.when(sector >= sector_count - 2)
    def _():
        clear(r_two)

    for t in range(3):
        prepare_tensor(0, t)
    widen_tensor(1)
    widen_mpo(1)
    for t in range(4):
        prepare_tensor(1, t)
    for side in range(2):
        for site in range(sites):
            for n in range(3):
                if (side, site, n) != (0, 0, 2):
                    prepare_mpo(side, site, n)

    both(0, lin, 0, 1, acc_one, False)
    loads[4].wait()
    both(1, rin, 1, 0, acc_right, False)

    r_own.start_all(jnp.logical_not(ahead))
    p_own.start_all(jnp.logical_not(ahead))
    s_own = pieces(s_send.at[0], s_recv.at[0], 2, {"sector": up})
    r_pass = pieces(r_one.at[0], r_two.at[0], 3, {"sector": down})

    def on_partial(c):
        p_own.wait_recv(c)
        emit(pitch, every, tall(c), acc_one, p_recv.at[0], s_send.at[0])
        s_own.start(c)

    def on_right(c):
        r_own.wait_recv(c)
        r_pass.start(c)

    in_order((bond_ends, on_right), (bra_ends, on_partial))
    both(0, lin, 0, 0, acc_zero, False)
    both(1, r_one.at[0], 1, 1, acc_right, True)

    def on_sum(c):
        s_own.wait_recv(c)
        emit(pitch, every, tall(c), acc_zero, s_recv.at[0], left_out.at[0])
        ket(0, left_out.at[0], 1, tall(c))

    def on_second_right(c):
        r_pass.wait_recv(c)
        first(1, r_two.at[0], 1, 2, wide(c), mid_bra)

    in_order((bond_ends, on_second_right), (bra_ends, on_sum))
    for stream in (r_own, p_own):
        stream.finish()
    early = (s_own, r_pass)

    p_own = pieces(p_send.at[1], p_recv.at[1], 5, {"sector": up})
    r_own = pieces(right_out.at[1], r_one.at[1], 4, {"sector": down})

    def send_partial(c):
        bra(0, 1, wide(c), None, p_send.at[1])
        p_own.start(c)

    def send_right(c):
        second(1, 1, 2, tall(c), mid_bra, acc_right, True)
        emit(pitch, every, tall(c), acc_right, None, right_out.at[1])
        r_own.start(c)

    in_order((bond_ends, send_partial), (bra_ends, send_right))

    both(0, left_out.at[0], 1, 1, acc_one, False)
    both(1, right_out.at[1], 0, 0, acc_right, False)
    s_own = pieces(s_send.at[1], s_recv.at[1], 6, {"sector": up})
    r_pass = pieces(r_one.at[1], r_two.at[1], 7, {"sector": down})
    edges = pieces(left_out.at[1], edge_out, 8, {"chain": after})

    def on_partial(c):
        p_own.wait_recv(c)
        emit(pitch, wide(c), whole, acc_one, p_recv.at[1], s_send.at[1])
        s_own.start(c)

    def on_right(c):
        r_own.wait_recv(c)
        r_pass.start(c)

    in_order((bra_ends, on_right), (bond_ends, on_partial))
    both(0, left_out.at[0], 1, 0, acc_zero, False)

    def on_sum(c):
        s_own.wait_recv(c)
        emit(pitch, wide(c), whole, acc_zero, s_recv.at[1], left_out.at[1])

        edges.start(c)

    def on_second_right(c):
        r_pass.wait_recv(c)
        ket(1, r_two.at[1], 0, tall(c))

    for stream in early + (r_own, p_own):
        stream.finish()
    on_sum(0)
    on_sum(1)
    on_sum(2)
    first(1, r_one.at[1], 0, 1, every, mid)
    on_sum(3)
    quarters = [(i * tile // 4, tile // 4) for i in range(4)]
    for i in range(2):
        second(1, 0, 1, quarters[i], mid, acc_right, True)
    on_sum(4)
    for i in range(2, 4):
        second(1, 0, 1, quarters[i], mid, acc_right, True)
    done = bond_ends[4]
    ends = [(end - done) / (1 - done) for end in bond_ends[5:]]

    def on_last_right(c):
        if c < SLICES:
            on_second_right(c)
        else:
            bra(1, 0, every, acc_right, right_out.at[0])

    lead = [LEAD * end for end in bra_ends] + [LEAD]
    in_order((lead, on_last_right), (ends, lambda c: on_sum(c + 5)))

    @pl.when(chain == 0)
    def _():
        keep_edge.wait()

    edges.wait_all()
    edges.finish()
    for stream in (s_own, r_pass):
        stream.finish()


def leave(left, right, edge):
    def body(left, right, edge, left_out, right_out, edge_out, sem):
        pairs = [(edge, edge_out.at[0, 0])]
        for src, dst in ((left, left_out), (right, right_out)):
            pairs += [(src.at[i], dst.at[i, 0]) for i in range(src.shape[0])]
        third = edge.shape[0] // PARTS
        cuts = [pl.ds(i * third, third) for i in range(PARTS)]
        pairs = [(src.at[cut], dst.at[cut]) for src, dst in pairs for cut in cuts]
        copies = [
            pltpu.make_async_copy(src, dst, sem.at[i])
            for i, (src, dst) in enumerate(pairs)
        ]
        for copy in copies:
            copy.start()
        for copy in copies:
            copy.wait()

    env = edge.shape
    sites = left.shape[0]
    hbm = pl.BlockSpec(memory_space=pl.ANY)
    return pl.pallas_call(
        body,
        out_shape=(
            jax.ShapeDtypeStruct((sites, 1) + env, left.dtype),
            jax.ShapeDtypeStruct((sites, 1) + env, left.dtype),
            jax.ShapeDtypeStruct((1, 1) + env, left.dtype),
        ),
        in_specs=[pl.BlockSpec(memory_space=pltpu.VMEM)] * 3,
        out_specs=[hbm] * 3,
        scratch_shapes=[pltpu.SemaphoreType.DMA((PARTS * (2 * sites + 1),))],
        compiler_params=pltpu.CompilerParams(vmem_limit_bytes=16 << 20),
    )(left, right, edge)


def shards(chain_count, sector_count, site_tensors, mpo, left_in, right_in, tile_rows):
    sites, _, tile, phys, _ = site_tensors.shape
    width = mpo.shape[1]
    padded = -(-width // 16) * 16
    pitch = tile + PITCH_EXTRA
    tensors = site_tensors.reshape(sites, tile * phys, tile)
    flat_mpo = mpo.transpose(0, 1, 3, 4, 2).reshape(sites, width * 16, width)
    env = (width, tile, tile)
    sizes = (chain_count, sector_count, sites, width, tile, padded, pitch)
    vmem = pl.BlockSpec(memory_space=pltpu.VMEM)
    hbm = pl.BlockSpec(memory_space=pl.ANY)
    left, right, edge = pl.pallas_call(
        functools.partial(kernel, sizes),
        out_shape=(
            pltpu.VMEM((sites,) + env, jnp.bfloat16),
            pltpu.VMEM((sites,) + env, jnp.bfloat16),
            pltpu.VMEM(env, jnp.bfloat16),
        ),
        in_specs=[hbm] * 5,
        out_specs=[vmem] * 3,
        scratch_shapes=[pltpu.VMEM(env, jnp.bfloat16)] * 2
        + [pltpu.VMEM((sites,) + env, jnp.bfloat16)] * 6
        + [
            pltpu.VMEM((2 * padded * pitch, tile), jnp.float32),
        ]
        + [pltpu.VMEM((padded * pitch, tile), jnp.float32)] * 6
        + [
            pltpu.VMEM((sites, phys, tile, tile), jnp.bfloat16),
            pltpu.VMEM((sites, phys, tile, tile), jnp.bfloat16),
            pltpu.VMEM((2, sites, 2, padded, tile), jnp.bfloat16),
            pltpu.VMEM((2, sites, 2 * padded, tile), jnp.bfloat16),
            pltpu.VMEM((sites, phys * tile, tile), jnp.bfloat16),
            pltpu.VMEM((sites, 16 * width, width), jnp.bfloat16),
            pltpu.VMEM((sites, phys * tile, tile), jnp.float32),
            pltpu.VMEM((sites, 16 * padded, tile), jnp.float32),
            pltpu.SMEM(tile_rows.shape, tile_rows.dtype),
            pltpu.SemaphoreType.DMA((9,)),
            pltpu.SemaphoreType.DMA((4 * SLICES + 5 * len(chunks_of(width)),)),
            pltpu.SemaphoreType.DMA((6,)),
        ],
        compiler_params=pltpu.CompilerParams(
            collective_id=0, has_side_effects=True, vmem_limit_bytes=52 << 20
        ),
    )(tile_rows, tensors, flat_mpo, left_in[0, 0], right_in[0, 0])
    return leave(left, right, edge)


def solution(mesh):
    envs = P("chain", "sector", None, None, None)
    return jax.shard_map(
        functools.partial(shards, mesh.shape["chain"], mesh.shape["sector"]),
        mesh=mesh,
        in_specs=(envs, P("chain", None, None, None, None), envs, envs, P()),
        out_specs=(envs, envs, envs),
        check_vma=False,
    )
```
